256 devices in a mesh: dp: 32 (over y_lo, z, core), proto: 8 (over x, y_hi).
Axes of the slice: x: 4, y: 4 (y_hi: 2, y_lo: 2; y = y_hi * 2 + y_lo), z: 8, core: 2. Of those that a mesh axis runs over, the one named last changes fastest.
Arguments:
- feature_matrix: bfloat16 [8192, 128], P('dp'), may hold values from -64 to 64
- tangent_embed: bfloat16 [8192, 128], P('dp'), may hold values from -2 to 2
- anchor_matrix: bfloat16 [65536, 128], P('proto'), may hold values from -4 to 4
- anchor_perturbation: bfloat16 [65536, 128], P('proto'), may hold values from -0.5 to 0.5
- codes: bfloat16 [8192, 65536], P('dp', 'proto'), may hold values from 0 to 3, as said below
- partner_lookup: int32 [8192], P('dp'), may hold values from 0 to 8191, as said below
Outputs:
- hvp_embed: bfloat16 [8192, 128], P('dp')
- hvp_proto: bfloat16 [65536, 128], P('proto')
The draws below stay inside these ranges and needn't reach their ends.
Inputs may be any that keep to these rules, and one draw needn't show every extreme that they name: partner_lookup[partner_lookup[i]] = i and partner_lookup[i] != i for every crop i. `codes`: positive.
All inputs are finite; a program needn't handle non-finite values.
Results may differ from the reference program's by a relative error of at most 0.0051.
Values may be sent and summed in bfloat16 or wider, within the bound.
No kernel may reach another device: no remote copies, remote signals or barrier semaphores. Data moves between devices by JAX's collectives and lax.ppermute only.
A program may use at most 128 MiB of HBM per device.

```python
import math
import jax
import jax.numpy as jnp
from jax import lax

D = 128
PROTOS = 65536
CROPS = 8192


def embed_pair(key):
    keys = jax.random.split(jax.random.fold_in(key, 7), 6)
    row_scale = jnp.exp(jax.random.uniform(keys[0], (CROPS, 1), jnp.float32, math.log(0.1), 0.0))
    col_scale = jnp.exp(jax.random.uniform(keys[1], (PROTOS, 1), jnp.float32, math.log(0.3), math.log(3.0)))
    raw_rows = jnp.clip(jax.random.normal(keys[4], (CROPS, D), jnp.float32), -6.0, 6.0)
    raw_cols = jnp.clip(jax.random.normal(keys[5], (PROTOS, D), jnp.float32), -6.0, 6.0)
    embed_values = row_scale * raw_rows
    proto_values = col_scale * raw_cols / math.sqrt(D)
    return (embed_values, proto_values)


def draw_feature_matrix(key, part):
    return embed_pair(key)[0].astype(jnp.bfloat16)


def draw_anchor_matrix(key, part):
    return embed_pair(key)[1].astype(jnp.bfloat16)


def draw_tangent_embed(key, part):
    keys = jax.random.split(jax.random.fold_in(key, 17), 3)
    values = jnp.clip(0.3 * jax.random.normal(keys[2], (CROPS, D), jnp.float32), -2.0, 2.0)
    return values.astype(jnp.bfloat16)


def draw_codes(key, part):
    keys = jax.random.split(jax.random.fold_in(key, 11), 2)
    raw = jnp.clip(jax.random.normal(keys[0], (CROPS, PROTOS), jnp.float32), -5.0, 5.0)
    row_factor = jnp.exp(jax.random.uniform(keys[1], (CROPS, 1), jnp.float32, math.log(0.3), math.log(3.0)))
    position = jnp.arange(PROTOS, dtype=jnp.float32)[None, :] / PROTOS
    trend = jnp.exp(math.log(3.0) * position)
    values = jnp.exp(0.5 * raw - 0.125) * row_factor * trend / PROTOS
    return values.astype(jnp.bfloat16)


def draw_partner_lookup(key, part):
    order = jax.random.permutation(jax.random.fold_in(key, 13), CROPS).astype(jnp.int32)
    partner = order.reshape(-1, 2)[:, ::-1].reshape(-1)
    return jnp.zeros((CROPS,), jnp.int32).at[order].set(partner)


def level_of(own_key, dims, shards, least, high):
    level, own = 1.0, jax.random.fold_in(own_key, 6)
    for dim, shards_of in shards:
        steps = jnp.exp(jax.random.uniform(jax.random.fold_in(own, dim), (shards_of,), jnp.float32, least / len(shards), high / len(shards)))
        level = level * jnp.repeat(steps, dims[dim] // shards_of).reshape([-1 if axis == dim else 1 for axis in range(len(dims))])
    return level


def centred(stream_key, extent, width, limit, cuts=(), held_as=jnp.bfloat16):
    values = jax.random.normal(stream_key, extent, jnp.float32) * width
    if len(cuts) > 0:
        values = level_of(stream_key, extent, cuts, -0.22, 0.18) * values
    return jnp.clip(values, min=-limit, max=limit).astype(held_as)


def setup_inputs(seed: int = 0) -> dict:
    splits = jax.random.split(jax.random.key(seed), 7)
    return {
        "feature_matrix": draw_feature_matrix(jax.random.fold_in(splits[6], 71), 0),
        "tangent_embed": draw_tangent_embed(jax.random.fold_in(splits[6], 71), 0),
        "anchor_matrix": draw_anchor_matrix(jax.random.fold_in(splits[6], 71), 0),
        "anchor_perturbation": centred(splits[3], (PROTOS, D), D ** -0.5, 0.5, ((0, 8),)),
        "codes": draw_codes(jax.random.fold_in(splits[6], 71), 0),
        "partner_lookup": draw_partner_lookup(jax.random.fold_in(splits[6], 71), 0),
    }


softening_constant = 0.1


def aggregated_elements(left, right):
    return lax.dot_general(left, right, (((1,), (1,)), ((), ())), preferred_element_type=jnp.float32)


def reduce_along_samples(left, right):
    return lax.dot_general(left, right, (((0,), (0,)), ((), ())), preferred_element_type=jnp.float32)


def reference(feature_matrix, tangent_embed, anchor_matrix, anchor_perturbation, codes, partner_lookup):
    traded_contributions = jnp.take(feature_matrix, partner_lookup, axis=0)
    swapped_tan = jnp.take(tangent_embed, partner_lookup, axis=0)
    tile_height = math.gcd(CROPS, 256)

    def one_block(running, block_index):
        sample_offset = (block_index * tile_height).astype(jnp.int32)
        traded_portion = lax.dynamic_slice_in_dim(traded_contributions, sample_offset, tile_height, 0)
        direction_piece = lax.dynamic_slice_in_dim(swapped_tan, sample_offset, tile_height, 0)
        code_piece = lax.dynamic_slice_in_dim(codes, sample_offset, tile_height, 0)
        unscaled_affinity = aggregated_elements(traded_portion, anchor_matrix) / softening_constant
        similarity_direction = (aggregated_elements(direction_piece, anchor_matrix) + aggregated_elements(traded_portion, anchor_perturbation)) / softening_constant
        highest = jnp.max(unscaled_affinity, axis=1, keepdims=True)
        exponent = jnp.exp(unscaled_affinity - highest)
        softmax_total = jnp.sum(exponent, axis=1, keepdims=True)
        weighted = jnp.sum(exponent * similarity_direction, axis=1, keepdims=True)
        line_sum_norm = jnp.sum(code_piece.astype(jnp.float32), axis=1, keepdims=True)
        model_likelihood = exponent / softmax_total
        mean_code_vector = weighted / softmax_total
        outer_patch_multiplier = (softening_constant * line_sum_norm * model_likelihood * (similarity_direction - mean_code_vector)).astype(jnp.bfloat16)
        right_crop_factor = (softening_constant * (line_sum_norm * model_likelihood - code_piece.astype(jnp.float32))).astype(jnp.bfloat16)
        hvp_rows = jnp.dot(outer_patch_multiplier, anchor_matrix, preferred_element_type=jnp.float32) + jnp.dot(right_crop_factor, anchor_perturbation, preferred_element_type=jnp.float32)
        running = running + reduce_along_samples(outer_patch_multiplier, traded_portion) + reduce_along_samples(right_crop_factor, direction_piece)
        return running, hvp_rows

    proto_sum, hvp_blocks = lax.scan(one_block, jnp.zeros((PROTOS, D), jnp.float32), jnp.arange(CROPS // tile_height, dtype=jnp.int32))
    hvp_swapped = hvp_blocks.reshape(CROPS, D).astype(jnp.bfloat16)
    return jnp.take(hvp_swapped, partner_lookup, axis=0), proto_sum.astype(jnp.bfloat16)
```

```python
import jax
import jax.numpy as jnp
from jax import lax
from jax.experimental import pallas as pl
from jax.experimental.pallas import tpu as pltpu
from jax.sharding import PartitionSpec as P

F32 = jnp.float32
BF16 = jnp.bfloat16
NT = (((1,), (1,)), ((), ()))
TN = (((0,), (0,)), ((), ()))
D = 128
ROWS = 256
LOCAL = 8192
DP = 32
PR = 8
SUB = ROWS // PR
CN = 2048
NCH = LOCAL // CN
SCALE = 0.1
VMEM = pl.BlockSpec(memory_space=pltpu.VMEM)
SMEM = pl.BlockSpec(memory_space=pltpu.SMEM)
GRANT = 56 * 1024 * 1024


def split3(x):
    hi = x.astype(BF16).astype(F32)
    mid = (x - hi).astype(BF16).astype(F32)
    lo = (x - hi - mid).astype(BF16).astype(F32)
    return hi, mid, lo


def codes_kernel(q_ref, codes_ref, pert_ref, tan_ref, h_ref, blk_ref, acc):
    step = pl.program_id(0)

    @pl.when(step == 0)
    def _():
        acc[...] = jnp.zeros_like(acc)

    rhs = jnp.concatenate([pert_ref[...], jnp.ones((CN, D), BF16)], axis=1)
    acc[...] += jnp.dot(codes_ref[...], rhs, preferred_element_type=F32)

    @pl.when(step == NCH - 1)
    def _():
        h_ref[...] = acc[:, :D]
        mass = jnp.transpose(acc[:, D:])[0:1, :]
        hi, mid, lo = split3(mass)
        parts = jnp.concatenate([hi, mid, lo, jnp.zeros((5, ROWS), F32)], axis=0)
        parts = jnp.concatenate([parts[:, :D], parts[:, D:]], axis=0).astype(BF16)
        rows = tan_ref[pl.ds(pl.multiple_of(q_ref[0] * SUB, SUB), SUB), :]
        block = jnp.concatenate([rows, parts], axis=0)
        for i in range(DP):
            blk_ref[i] = block


def codes_pass(q, codes, pert, tan):
    return pl.pallas_call(
        codes_kernel,
        grid=(NCH,),
        in_specs=[
            SMEM,
            pl.BlockSpec((ROWS, CN), lambda c: (0, c)),
            pl.BlockSpec((CN, D), lambda c: (c, 0)),
            pl.BlockSpec((ROWS, D), lambda c: (0, 0)),
        ],
        out_specs=[
            pl.BlockSpec((ROWS, D), lambda c: (0, 0)),
            pl.BlockSpec((DP, SUB + 16, D), lambda c: (0, 0, 0)),
        ],
        out_shape=[
            jax.ShapeDtypeStruct((ROWS, D), F32),
            jax.ShapeDtypeStruct((DP, SUB + 16, D), BF16),
        ],
        scratch_shapes=[pltpu.VMEM((ROWS, 2 * D), F32)],
        cost_estimate=pl.CostEstimate(flops=2 * ROWS * LOCAL * 256, bytes_accessed=7 << 20, transcendentals=0),
        name="codes_pass",
    )(q, codes, pert, tan)


RG = 16


def score_kernel(f_ref, tan_ref, a_ref, p_ref, e_ref, u_ref, cst_ref, st_ref, x_ref, w_ref, s_sc, t_sc, run):
    step = pl.program_id(0)
    f = f_ref[...]
    s_sc[...] = lax.dot_general(f, a_ref[...], NT, preferred_element_type=F32)
    left = jnp.concatenate([tan_ref[...], f], axis=1)
    right = jnp.concatenate([a_ref[...], p_ref[...]], axis=1)
    t_sc[...] = lax.dot_general(left, right, NT, preferred_element_type=F32)

    @pl.when(step == 0)
    def _():
        run[0] = jnp.full((ROWS, D), -jnp.inf, F32)
        run[1] = jnp.zeros((ROWS, D), F32)
        run[2] = jnp.zeros((ROWS, D), F32)
        x_ref[...] = jnp.zeros_like(x_ref)
        w_ref[...] = jnp.zeros_like(w_ref)

    for g in range(ROWS // RG):
        rows = slice(g * RG, (g + 1) * RG)
        s = s_sc[rows, :]
        t = t_sc[rows, :] * (1.0 / SCALE)
        top = jnp.max(s, axis=1, keepdims=True)
        e = jnp.exp((s - top) * (1.0 / SCALE))
        z = jnp.sum(e, axis=1, keepdims=True)
        et = jnp.sum(e * t, axis=1, keepdims=True)
        mean = et / z
        e_ref[rows, :] = e.astype(BF16)
        u_ref[rows, :] = (e * (t - mean)).astype(BF16)
        lane = lax.broadcasted_iota(jnp.int32, (RG, D), 1)
        cst_ref[0, rows, :] = jnp.where(lane == 0, top * (1.0 / SCALE), mean)
        run_new = jnp.broadcast_to(z, (RG, D))
        st_ref[0, rows, :] = jnp.broadcast_to(top * (1.0 / SCALE), (RG, D))
        st_ref[1, rows, :] = run_new
        st_ref[2, rows, :] = jnp.broadcast_to(et, (RG, D))

    top = st_ref[0]
    z = st_ref[1]
    et = st_ref[2]
    mean = et / z
    old = run[0]
    new = jnp.maximum(old, top)
    alpha = jnp.exp(old - new)
    beta = jnp.exp(top - new)
    e = e_ref[...]
    ea = jnp.dot(e, a_ref[...], preferred_element_type=F32)
    ep = jnp.dot(e, p_ref[...], preferred_element_type=F32)
    ua = jnp.dot(u_ref[...], a_ref[...], preferred_element_type=F32)
    x_ref[...] = x_ref[...] * alpha + beta * (ua + ep + mean * ea)
    w_ref[...] = w_ref[...] * alpha + beta * ea
    run[0] = new
    run[1] = run[1] * alpha + beta * z
    run[2] = run[2] * alpha + beta * et
    st_ref[...] = run[...]


def score_pass(f, tan, a, p):
    return pl.pallas_call(
        score_kernel,
        grid=(NCH,),
        in_specs=[
            pl.BlockSpec((ROWS, D), lambda c: (0, 0)),
            pl.BlockSpec((ROWS, D), lambda c: (0, 0)),
            pl.BlockSpec((CN, D), lambda c: (c, 0)),
            pl.BlockSpec((CN, D), lambda c: (c, 0)),
        ],
        out_specs=[
            pl.BlockSpec((ROWS, CN), lambda c: (0, c)),
            pl.BlockSpec((ROWS, CN), lambda c: (0, c)),
            pl.BlockSpec((1, ROWS, D), lambda c: (c, 0, 0)),
            pl.BlockSpec((3, ROWS, D), lambda c: (0, 0, 0)),
            pl.BlockSpec((ROWS, D), lambda c: (0, 0)),
            pl.BlockSpec((ROWS, D), lambda c: (0, 0)),
        ],
        out_shape=[
            jax.ShapeDtypeStruct((ROWS, LOCAL), BF16),
            jax.ShapeDtypeStruct((ROWS, LOCAL), BF16),
            jax.ShapeDtypeStruct((NCH, ROWS, D), F32),
            jax.ShapeDtypeStruct((3, ROWS, D), F32),
            jax.ShapeDtypeStruct((ROWS, D), F32),
            jax.ShapeDtypeStruct((ROWS, D), F32),
        ],
        scratch_shapes=[
            pltpu.VMEM((ROWS, CN), F32),
            pltpu.VMEM((ROWS, CN), F32),
            pltpu.VMEM((3, ROWS, D), F32),
        ],
        compiler_params=pltpu.CompilerParams(vmem_limit_bytes=GRANT),
        cost_estimate=pl.CostEstimate(flops=14 * ROWS * LOCAL * D * 2, bytes_accessed=12 << 20, transcendentals=ROWS * LOCAL),
        name="score_pass",
    )(f, tan, a, p)


STAT = 16


def pick_kernel(q_ref, tab_ref, part_ref, st_ref, pay_ref):
    q = q_ref[0]
    partner = part_ref[...]
    group = partner // ROWS
    row = partner % ROWS
    mine = (row // SUB) == q
    column = jnp.where(mine, group * SUB + row % SUB, -1)
    hot = (lax.broadcasted_iota(jnp.int32, (ROWS, DP * SUB), 1) == column).astype(F32).astype(BF16)
    table = tab_ref[:, :SUB, :].reshape(DP * SUB, D)
    rows = jnp.dot(hot, table, preferred_element_type=F32).astype(BF16)

    hot_group = (lax.broadcasted_iota(jnp.int32, (ROWS, DP), 1) == group).astype(F32).astype(BF16)
    mass_rows = tab_ref[:, SUB:, :].astype(F32)
    mass = jnp.zeros((ROWS, ROWS), F32)
    for k in (2, 1, 0):
        piece = jnp.concatenate([mass_rows[:, k, :], mass_rows[:, 8 + k, :]], axis=1).astype(BF16)
        mass = mass + jnp.dot(hot_group, piece, preferred_element_type=F32)
    here = lax.broadcasted_iota(jnp.int32, (ROWS, ROWS), 1) == row
    mass = jnp.sum(jnp.where(here, mass, 0.0), axis=1, keepdims=True)

    lane = lax.broadcasted_iota(jnp.int32, (ROWS, D), 1)
    values = (st_ref[0], st_ref[1], st_ref[2], jnp.broadcast_to(mass, (ROWS, D)))
    cols = jnp.zeros((ROWS, D), F32)
    for v, value in enumerate(values):
        for k, piece in enumerate(split3(value)):
            cols = jnp.where(lane == v * 3 + k, piece, cols)
    flat = jnp.transpose(cols)[:STAT, :]
    flat = jnp.concatenate([flat[:, :D], flat[:, D:]], axis=0).astype(BF16)
    payload = jnp.concatenate([rows, flat], axis=0)
    for i in range(PR):
        pay_ref[i] = payload


def pick(q, tab, partner, st):
    return pl.pallas_call(
        pick_kernel,
        in_specs=[SMEM, VMEM, VMEM, VMEM],
        out_specs=VMEM,
        out_shape=jax.ShapeDtypeStruct((PR, ROWS + 2 * STAT, D), BF16),
        compiler_params=pltpu.CompilerParams(vmem_limit_bytes=GRANT),
        name="pick",
    )(q, tab, partner, st)


def proto_kernel(c_ref, rec_ref, f_ref, tan_ref, st_ref, cst_ref, x_ref, w_ref, u_ref, e_ref, codes_ref,
                 mine_ref, send_ref, emb_ref, coef, swt):
    step = pl.program_id(0)

    @pl.when(step == 0)
    def _():
        total = jnp.zeros((ROWS, D), F32)
        flats = []
        for i in range(PR):
            total = total + rec_ref[i, :ROWS, :].astype(F32)
            flat = rec_ref[i, ROWS:, :].astype(F32)
            flats.append(jnp.concatenate([flat[:STAT], flat[STAT:]], axis=1))
        swt[...] = (total * SCALE).astype(BF16)
        cols = jnp.transpose(jnp.concatenate(flats, axis=0))
        value = [[(cols[:, i * STAT + 3 * v : i * STAT + 3 * v + 1]
                   + cols[:, i * STAT + 3 * v + 1 : i * STAT + 3 * v + 2])
                  + cols[:, i * STAT + 3 * v + 2 : i * STAT + 3 * v + 3] for v in range(4)] for i in range(PR)]
        top = value[0][0]
        for i in range(1, PR):
            top = jnp.maximum(top, value[i][0])
        z = jnp.zeros((ROWS, 1), F32)
        et = jnp.zeros((ROWS, 1), F32)
        mass = jnp.zeros((ROWS, 1), F32)
        for i in range(PR):
            shift = jnp.exp(value[i][0] - top)
            z = z + shift * value[i][1]
            et = et + shift * value[i][2]
            mass = mass + value[i][3]
        mean = et / z
        weight = SCALE * mass / z
        top = jnp.broadcast_to(top, (ROWS, D))
        mean = jnp.broadcast_to(mean, (ROWS, D))
        weight = jnp.broadcast_to(weight, (ROWS, D))
        coef[0] = top
        coef[1] = mean
        coef[2] = weight
        emb_ref[...] = weight * jnp.exp(st_ref[0] - top) * (x_ref[...] - mean * w_ref[...])

    f = f_ref[...].astype(F32)
    tan = tan_ref[...].astype(F32)
    top_c = jnp.broadcast_to(cst_ref[0, :, 0:1], (ROWS, D))
    mean_c = jnp.broadcast_to(cst_ref[0, :, 1:2], (ROWS, D))
    weight = coef[2] * jnp.exp(top_c - coef[0])
    f1 = (weight * f).astype(BF16)
    f2 = (weight * ((mean_c - coef[1]) * f + tan)).astype(BF16)
    res = lax.dot_general(u_ref[...], f1, TN, preferred_element_type=F32)
    res = res + lax.dot_general(e_ref[...], f2, TN, preferred_element_type=F32)
    res = res - lax.dot_general(codes_ref[...], swt[...], TN, preferred_element_type=F32)
    first = c_ref[0] == 0
    for b in range(CN // (2 * ROWS)):
        even = res[2 * b * ROWS : (2 * b + 1) * ROWS]
        odd = res[(2 * b + 1) * ROWS : (2 * b + 2) * ROWS]
        mine_ref[b] = jnp.where(first, even, odd)
        send_ref[b] = jnp.where(first, odd, even).astype(BF16)


def proto_pass(core, rec, f, tan, st, cst, x, w, u, e, codes):
    nb = CN // (2 * ROWS)
    whole2 = pl.BlockSpec((ROWS, D), lambda c: (0, 0))
    return pl.pallas_call(
        proto_kernel,
        grid=(NCH,),
        in_specs=[
            SMEM,
            pl.BlockSpec((PR, ROWS + 2 * STAT, D), lambda c: (0, 0, 0)),
            whole2,
            whole2,
            pl.BlockSpec((3, ROWS, D), lambda c: (0, 0, 0)),
            pl.BlockSpec((1, ROWS, D), lambda c: (c, 0, 0)),
            whole2,
            whole2,
            pl.BlockSpec((ROWS, CN), lambda c: (0, c)),
            pl.BlockSpec((ROWS, CN), lambda c: (0, c)),
            pl.BlockSpec((ROWS, CN), lambda c: (0, c)),
        ],
        out_specs=[
            pl.BlockSpec((nb, ROWS, D), lambda c: (c, 0, 0)),
            pl.BlockSpec((nb, ROWS, D), lambda c: (c, 0, 0)),
            pl.BlockSpec((ROWS, D), lambda c: (0, 0)),
        ],
        out_shape=[
            jax.ShapeDtypeStruct((16, ROWS, D), F32),
            jax.ShapeDtypeStruct((16, ROWS, D), BF16),
            jax.ShapeDtypeStruct((ROWS, D), F32),
        ],
        scratch_shapes=[pltpu.VMEM((3, ROWS, D), F32), pltpu.VMEM((ROWS, D), BF16)],
        compiler_params=pltpu.CompilerParams(vmem_limit_bytes=GRANT),
        cost_estimate=pl.CostEstimate(flops=6 * ROWS * LOCAL * D * 2, bytes_accessed=15 << 20, transcendentals=0),
        name="proto_pass",
    )(core, rec, f, tan, st, cst, x, w, u, e, codes)


CORE_PERM = [(i, i ^ 1) for i in range(DP)]
Y_PERM = [(i, i ^ 16) for i in range(DP)]
Z_GROUPS = [[y * 16 + z * 2 + c for z in range(8)] for y in range(2) for c in range(2)]


def exchange(x, axis, groups=None):
    return lax.all_to_all(x, axis, 0, 0, axis_index_groups=groups, tiled=True)


def body(feature_matrix, tangent_embed, anchor_matrix, anchor_perturbation, codes, partner_lookup):
    dp = lax.axis_index("dp")
    q = lax.axis_index("proto")
    core = dp % 2
    y = dp // 16
    partner = partner_lookup.reshape(ROWS, 1)
    qs = q.reshape(1)

    h_part, block = codes_pass(qs, codes, anchor_perturbation, tangent_embed)
    table = exchange(block, "dp")
    e, u, cst, st, x, w = score_pass(feature_matrix, tangent_embed, anchor_matrix, anchor_perturbation)
    h_rows = jnp.sum(exchange(h_part.reshape(PR, SUB, D), "proto"), axis=0)
    h_table = exchange(jnp.broadcast_to(h_rows.astype(BF16)[None], (DP, SUB, D)), "dp").reshape(DP * SUB, D)

    payload = pick(qs, table, partner, st)
    received = exchange(payload, "proto")
    mine, send, embed = proto_pass(core.reshape(1), received, feature_matrix, tangent_embed, st, cst, x, w, u, e, codes)

    got = lax.ppermute(send, "dp", CORE_PERM)
    half = (mine + got.astype(F32)).reshape(2, 8, ROWS, D)
    other = lax.dynamic_index_in_dim(half, 1 - y, 0, keepdims=False).astype(BF16)
    own = lax.dynamic_index_in_dim(half, y, 0, keepdims=False)
    quarter = own + lax.ppermute(other, "dp", Y_PERM).astype(F32)
    pieces = exchange(quarter.astype(BF16), "dp", Z_GROUPS)
    final = jnp.sum(pieces.astype(F32), axis=0).astype(BF16)

    along_z = exchange(jnp.broadcast_to(final[None], (8, ROWS, D)), "dp", Z_GROUPS)
    from_y = lax.ppermute(along_z, "dp", Y_PERM)
    plane = jnp.where(y == 0, jnp.stack([along_z, from_y]), jnp.stack([from_y, along_z])).reshape(16, ROWS, D)
    from_core = lax.ppermute(plane, "dp", CORE_PERM)
    pair = jnp.where(core == 0, jnp.stack([plane, from_core], 1), jnp.stack([from_core, plane], 1))
    hvp_proto = pair.reshape(LOCAL, D)

    group = partner // ROWS
    row = partner % ROWS
    column = jnp.where(row // SUB == q, group * SUB + row % SUB, -1)
    hot = (lax.broadcasted_iota(jnp.int32, (ROWS, DP * SUB), 1) == column).astype(BF16)
    h_mine = jnp.dot(hot, h_table, preferred_element_type=F32)
    embed = embed - SCALE * h_mine
    part = jnp.sum(exchange(embed.reshape(PR, SUB, D), "proto"), axis=0).astype(BF16)
    hvp_embed = exchange(jnp.broadcast_to(part[None], (PR, SUB, D)), "proto").reshape(ROWS, D)
    return (hvp_embed, hvp_proto)


def solution(mesh):
    in_specs = (
        P("dp", None),
        P("dp", None),
        P("proto", None),
        P("proto", None),
        P("dp", "proto"),
        P("dp"),
    )
    out_specs = (P("dp", None), P("proto", None))
    return jax.shard_map(body, mesh=mesh, in_specs=in_specs, out_specs=out_specs, check_vma=False)
```

```python
import jax
import jax.numpy as jnp
from jax import lax
from jax.experimental import pallas as pl
from jax.experimental.pallas import tpu as pltpu
from jax.sharding import PartitionSpec as P

F32 = jnp.float32
BF16 = jnp.bfloat16
NT = (((1,), (1,)), ((), ()))
TN = (((0,), (0,)), ((), ()))
D = 128
ROWS = 256
LOCAL = 8192
DP = 32
PR = 8
SUB = ROWS // PR
CN = 2048
NCH = LOCAL // CN
SCALE = 0.1
RG = 16
INV = 10.0
LOG2E = 1.4426950408889634
VMEM = pl.BlockSpec(memory_space=pltpu.VMEM)
SMEM = pl.BlockSpec(memory_space=pltpu.SMEM)
GRANT = 56 * 1024 * 1024


def split3(x):
    hi = x.astype(BF16).astype(F32)
    mid = (x - hi).astype(BF16).astype(F32)
    lo = (x - hi - mid).astype(BF16).astype(F32)
    return hi, mid, lo


def mass_kernel(q_ref, codes_ref, tan_ref, blk_ref, acc):
    step = pl.program_id(0)

    @pl.when(step == 0)
    def _():
        acc[...] = jnp.zeros_like(acc)

    for g in range(ROWS // RG):
        rows = slice(g * RG, (g + 1) * RG)
        x = codes_ref[rows, :].astype(F32)
        total = x[:, :D]
        for k in range(1, CN // D):
            total = total + x[:, k * D : (k + 1) * D]
        acc[rows, :] += total

    @pl.when(step == NCH - 1)
    def _():
        mass = jnp.sum(jnp.transpose(acc[...]), axis=0, keepdims=True)
        hi, mid, lo = split3(mass)
        parts = jnp.concatenate([hi, mid, lo, jnp.zeros((5, ROWS), F32)], axis=0)
        parts = jnp.concatenate([parts[:, :D], parts[:, D:]], axis=0).astype(BF16)
        rows = tan_ref[pl.ds(pl.multiple_of(q_ref[0] * SUB, SUB), SUB), :]
        block = jnp.concatenate([rows, parts], axis=0)
        for i in range(DP):
            blk_ref[i] = block


def mass_pass(q, codes, tan):
    return pl.pallas_call(
        mass_kernel,
        grid=(NCH,),
        in_specs=[
            SMEM,
            pl.BlockSpec((ROWS, CN), lambda c: (0, c)),
            pl.BlockSpec((ROWS, D), lambda c: (0, 0)),
        ],
        out_specs=pl.BlockSpec((DP, SUB + 16, D), lambda c: (0, 0, 0)),
        out_shape=jax.ShapeDtypeStruct((DP, SUB + 16, D), BF16),
        scratch_shapes=[pltpu.VMEM((ROWS, D), F32)],
        cost_estimate=pl.CostEstimate(flops=ROWS * LOCAL, bytes_accessed=5 << 20, transcendentals=0),
        name="mass_pass",
    )(q, codes, tan)


def h_kernel(codes_ref, pert_ref, h_ref, acc):
    step = pl.program_id(0)

    @pl.when(step == 0)
    def _():
        acc[...] = jnp.zeros_like(acc)

    acc[...] += jnp.dot(codes_ref[...], pert_ref[...], preferred_element_type=F32)

    @pl.when(step == NCH - 1)
    def _():
        h_ref[...] = acc[...].astype(BF16)


def h_pass(codes, pert):
    return pl.pallas_call(
        h_kernel,
        grid=(NCH,),
        in_specs=[
            pl.BlockSpec((ROWS, CN), lambda c: (0, c)),
            pl.BlockSpec((CN, D), lambda c: (c, 0)),
        ],
        out_specs=pl.BlockSpec((ROWS, D), lambda c: (0, 0)),
        out_shape=jax.ShapeDtypeStruct((ROWS, D), BF16),
        scratch_shapes=[pltpu.VMEM((ROWS, D), F32)],
        cost_estimate=pl.CostEstimate(flops=2 * ROWS * LOCAL * D * 2, bytes_accessed=7 << 20, transcendentals=0),
        name="h_pass",
    )(codes, pert)


def score_kernel(f_ref, tan_ref, a_ref, p_ref, e_ref, u_ref, cst_ref, st_ref, s_sc, t_sc, run):
    step = pl.program_id(0)
    f = f_ref[...]
    s_sc[...] = lax.dot_general(f, a_ref[...], NT, preferred_element_type=F32)
    left = jnp.concatenate([tan_ref[...], f], axis=1)
    right = jnp.concatenate([a_ref[...], p_ref[...]], axis=1)
    t_sc[...] = lax.dot_general(left, right, NT, preferred_element_type=F32)

    @pl.when(step == 0)
    def _():
        run[0] = jnp.full((ROWS, D), -jnp.inf, F32)
        run[1] = jnp.zeros((ROWS, D), F32)
        run[2] = jnp.zeros((ROWS, D), F32)

    lane = lax.broadcasted_iota(jnp.int32, (RG, D), 1)
    for g in range(ROWS // RG):
        rows = slice(g * RG, (g + 1) * RG)
        s = s_sc[rows, :]
        t = t_sc[rows, :]
        top = jnp.max(s, axis=1, keepdims=True)
        e = jnp.exp2((s - top) * (INV * LOG2E))
        z = jnp.sum(e, axis=1, keepdims=True)
        et = jnp.sum(e * t, axis=1, keepdims=True)
        mean = et / z
        e_ref[rows, :] = e.astype(BF16)
        u_ref[rows, :] = (e * (t - mean)).astype(BF16)
        top = top * INV
        cst_ref[0, rows, :] = jnp.where(lane == 0, top, mean * INV)
        old = run[0, rows, :]
        new = jnp.maximum(old, top)
        alpha = jnp.exp(old - new)
        beta = jnp.exp(top - new)
        z_run = run[1, rows, :] * alpha + beta * z
        et_run = run[2, rows, :] * alpha + beta * (et * INV)
        run[0, rows, :] = new
        run[1, rows, :] = z_run
        run[2, rows, :] = et_run
        st_ref[rows, :] = jnp.where(lane == 0, new, jnp.where(lane == 1, z_run, et_run))


def score_pass(f, tan, a, p):
    return pl.pallas_call(
        score_kernel,
        grid=(NCH,),
        in_specs=[
            pl.BlockSpec((ROWS, D), lambda c: (0, 0)),
            pl.BlockSpec((ROWS, D), lambda c: (0, 0)),
            pl.BlockSpec((CN, D), lambda c: (c, 0)),
            pl.BlockSpec((CN, D), lambda c: (c, 0)),
        ],
        out_specs=[
            pl.BlockSpec((ROWS, CN), lambda c: (0, c)),
            pl.BlockSpec((ROWS, CN), lambda c: (0, c)),
            pl.BlockSpec((1, ROWS, D), lambda c: (c, 0, 0)),
            pl.BlockSpec((ROWS, D), lambda c: (0, 0)),
        ],
        out_shape=[
            jax.ShapeDtypeStruct((ROWS, LOCAL), BF16),
            jax.ShapeDtypeStruct((ROWS, LOCAL), BF16),
            jax.ShapeDtypeStruct((NCH, ROWS, D), F32),
            jax.ShapeDtypeStruct((ROWS, D), F32),
        ],
        scratch_shapes=[
            pltpu.VMEM((ROWS, CN), F32),
            pltpu.VMEM((ROWS, CN), F32),
            pltpu.VMEM((3, ROWS, D), F32),
        ],
        cost_estimate=pl.CostEstimate(flops=10 * ROWS * LOCAL * D * 2, bytes_accessed=12 << 20, transcendentals=ROWS * LOCAL),
        name="score_pass",
    )(f, tan, a, p)


def embed_kernel(e_ref, u_ref, a_ref, p_ref, cst_ref, st_ref, x_ref, w_ref):
    @pl.when(pl.program_id(0) == 0)
    def _():
        x_ref[...] = jnp.zeros_like(x_ref)
        w_ref[...] = jnp.zeros_like(w_ref)

    e = e_ref[...]
    both = jnp.dot(e, jnp.concatenate([a_ref[...], p_ref[...]], axis=1), preferred_element_type=F32)
    ua = jnp.dot(u_ref[...], a_ref[...], preferred_element_type=F32)
    ea = both[:, :D]
    beta = jnp.exp(cst_ref[0, :, 0:1] - st_ref[:, 0:1])
    mean = cst_ref[0, :, 1:2]
    x_ref[...] += beta * (INV * ua + both[:, D:] + mean * ea)
    w_ref[...] += beta * ea


def embed_pass(e, u, a, p, cst, st):
    return pl.pallas_call(
        embed_kernel,
        grid=(NCH,),
        in_specs=[
            pl.BlockSpec((ROWS, CN), lambda c: (0, c)),
            pl.BlockSpec((ROWS, CN), lambda c: (0, c)),
            pl.BlockSpec((CN, D), lambda c: (c, 0)),
            pl.BlockSpec((CN, D), lambda c: (c, 0)),
            pl.BlockSpec((1, ROWS, D), lambda c: (c, 0, 0)),
            pl.BlockSpec((ROWS, D), lambda c: (0, 0)),
        ],
        out_specs=[
            pl.BlockSpec((ROWS, D), lambda c: (0, 0)),
            pl.BlockSpec((ROWS, D), lambda c: (0, 0)),
        ],
        out_shape=[jax.ShapeDtypeStruct((ROWS, D), F32)] * 2,
        cost_estimate=pl.CostEstimate(flops=6 * ROWS * LOCAL * D * 2, bytes_accessed=12 << 20, transcendentals=0),
        name="embed_pass",
    )(e, u, a, p, cst, st)


STAT = 16
PAY = ROWS + 2 * STAT + SUB


def pick_kernel(q_ref, tab_ref, part_ref, st_ref, h_ref, pay_ref):
    q = q_ref[0]
    partner = part_ref[...]
    group = partner // ROWS
    row = partner % ROWS
    mine = (row // SUB) == q
    column = jnp.where(mine, group * SUB + row % SUB, -1)
    hot = (lax.broadcasted_iota(jnp.int32, (ROWS, DP * SUB), 1) == column).astype(F32).astype(BF16)
    table = tab_ref[:, :SUB, :].reshape(DP * SUB, D)
    rows = jnp.dot(hot, table, preferred_element_type=F32).astype(BF16)

    hot_group = (lax.broadcasted_iota(jnp.int32, (ROWS, DP), 1) == group).astype(F32).astype(BF16)
    mass_rows = tab_ref[:, SUB:, :].astype(F32)
    mass = jnp.zeros((ROWS, ROWS), F32)
    for k in (2, 1, 0):
        piece = jnp.concatenate([mass_rows[:, k, :], mass_rows[:, 8 + k, :]], axis=1).astype(BF16)
        mass = mass + jnp.dot(hot_group, piece, preferred_element_type=F32)
    here = lax.broadcasted_iota(jnp.int32, (ROWS, ROWS), 1) == row
    mass = jnp.sum(jnp.where(here, mass, 0.0), axis=1, keepdims=True)

    lane = lax.broadcasted_iota(jnp.int32, (ROWS, D), 1)
    stats = jnp.where(lane == 3, mass, st_ref[...])
    flat = jnp.transpose(stats)[:4, :]
    hi, mid, lo = split3(flat)
    flat = jnp.concatenate([hi, mid, lo, jnp.zeros((STAT - 12, ROWS), F32)], axis=0)
    flat = jnp.concatenate([flat[:, :D], flat[:, D:]], axis=0).astype(BF16)
    payload = jnp.concatenate([rows, flat], axis=0)
    for i in range(PR):
        pay_ref[i, : ROWS + 2 * STAT, :] = payload
        pay_ref[i, ROWS + 2 * STAT :, :] = h_ref[i * SUB : (i + 1) * SUB, :]


def pick(q, tab, partner, st, h):
    return pl.pallas_call(
        pick_kernel,
        in_specs=[SMEM, VMEM, VMEM, VMEM, VMEM],
        out_specs=VMEM,
        out_shape=jax.ShapeDtypeStruct((PR, PAY, D), BF16),
        name="pick",
    )(q, tab, partner, st, h)


def stats_kernel(rec_ref, f_ref, tan_ref, st_ref, cst_ref, f12_ref, swt_ref, gst_ref, h_ref):
    total = jnp.zeros((ROWS, D), F32)
    h = jnp.zeros((SUB, D), F32)
    flats = []
    for i in range(PR):
        total = total + rec_ref[i, :ROWS, :].astype(F32)
        flat = rec_ref[i, ROWS : ROWS + 2 * STAT, :].astype(F32)
        flat = jnp.concatenate([flat[:STAT], flat[STAT:]], axis=1)
        flats.append((flat[0:4] + flat[4:8]) + flat[8:12])
        h = h + rec_ref[i, ROWS + 2 * STAT :, :].astype(F32)
    swt_ref[...] = (total * SCALE).astype(BF16)
    h_ref[...] = h.astype(BF16)
    top = flats[0][0:1]
    for i in range(1, PR):
        top = jnp.maximum(top, flats[i][0:1])
    z = jnp.zeros((1, ROWS), F32)
    et = jnp.zeros((1, ROWS), F32)
    mass = jnp.zeros((1, ROWS), F32)
    for i in range(PR):
        shift = jnp.exp(flats[i][0:1] - top)
        z = z + shift * flats[i][1:2]
        et = et + shift * flats[i][2:3]
        mass = mass + flats[i][3:4]
    rows = jnp.concatenate([top, et / z, SCALE * mass / z, jnp.zeros((D - 3, ROWS), F32)], axis=0)
    cols = jnp.transpose(rows)
    gst_ref[...] = cols
    top = cols[:, 0:1]
    mean = cols[:, 1:2]
    weight = cols[:, 2:3]
    f = f_ref[...].astype(F32)
    tan = tan_ref[...].astype(F32)
    for c in range(NCH):
        scale = weight * jnp.exp(cst_ref[c, :, 0:1] - top)
        f12_ref[c, :, :D] = (INV * scale * f).astype(BF16)
        f12_ref[c, :, D:] = (scale * ((cst_ref[c, :, 1:2] - mean) * f + tan)).astype(BF16)


def stats_pass(rec, f, tan, st, cst):
    return pl.pallas_call(
        stats_kernel,
        in_specs=[VMEM] * 5,
        out_specs=[VMEM] * 4,
        out_shape=[
            jax.ShapeDtypeStruct((NCH, ROWS, 2 * D), BF16),
            jax.ShapeDtypeStruct((ROWS, D), BF16),
            jax.ShapeDtypeStruct((ROWS, D), F32),
            jax.ShapeDtypeStruct((SUB, D), BF16),
        ],
        name="stats_pass",
    )(rec, f, tan, st, cst)


def proto_kernel(s_ref, f12_ref, swt_ref, u_ref, e_ref, codes_ref, mine_ref, send_ref):
    f12 = f12_ref[0]
    res = lax.dot_general(u_ref[...], f12[:, :D], TN, preferred_element_type=F32)
    res = res + lax.dot_general(e_ref[...], f12[:, D:], TN, preferred_element_type=F32)
    res = res - lax.dot_general(codes_ref[...], swt_ref[...], TN, preferred_element_type=F32)
    first = s_ref[0] == 0
    for b in range(CN // (2 * ROWS)):
        even = res[2 * b * ROWS : (2 * b + 1) * ROWS]
        odd = res[(2 * b + 1) * ROWS : (2 * b + 2) * ROWS]
        mine_ref[b] = jnp.where(first, even, odd)
        send_ref[b] = jnp.where(first, odd, even).astype(BF16)


def proto_pass(scalars, f12, swt, u, e, codes):
    nb = CN // (2 * ROWS)
    steps = NCH // 2
    wide = pl.BlockSpec((ROWS, CN), lambda c, s: (0, s[1] * steps + c))
    return pl.pallas_call(
        proto_kernel,
        grid_spec=pltpu.PrefetchScalarGridSpec(
            num_scalar_prefetch=1,
            grid=(steps,),
            in_specs=[
                pl.BlockSpec((1, ROWS, 2 * D), lambda c, s: (s[1] * steps + c, 0, 0)),
                pl.BlockSpec((ROWS, D), lambda c, s: (0, 0)),
                wide,
                wide,
                wide,
            ],
            out_specs=[
                pl.BlockSpec((nb, ROWS, D), lambda c, s: (c, 0, 0)),
                pl.BlockSpec((nb, ROWS, D), lambda c, s: (c, 0, 0)),
            ],
        ),
        out_shape=[
            jax.ShapeDtypeStruct((8, ROWS, D), F32),
            jax.ShapeDtypeStruct((8, ROWS, D), BF16),
        ],
        cost_estimate=pl.CostEstimate(flops=3 * ROWS * LOCAL * D * 2, bytes_accessed=9 << 20, transcendentals=0),
        name="proto_pass",
    )(scalars, f12, swt, u, e, codes)


HR = 4 * SUB


def final_kernel(s_ref, pieces_ref, part_ref, x_ref, w_ref, st_ref, gst_ref, out_ref, emb_ref):
    total = pieces_ref[0, :ROWS, :].astype(F32)
    for i in range(1, 8):
        total = total + pieces_ref[i, :ROWS, :].astype(F32)
    total = total.astype(BF16)
    for i in range(8):
        out_ref[i] = total
    q = s_ref[0]
    core = s_ref[1]
    y = s_ref[2]
    partner = part_ref[...]
    group = partner // ROWS
    row = partner % ROWS
    c_rel = jnp.where(group % 2 == core, 0, 1)
    y_rel = jnp.where(group // 16 == y, 0, 1)
    column = ((group // 2) % 8) * HR + (y_rel * 2 + c_rel) * SUB + row % SUB
    column = jnp.where((row // SUB) == q, column, -1)
    hot = (lax.broadcasted_iota(jnp.int32, (ROWS, 8 * HR), 1) == column).astype(F32).astype(BF16)
    table = pieces_ref[:, ROWS:, :].reshape(8 * HR, D)
    h = jnp.dot(hot, table, preferred_element_type=F32)
    scale = gst_ref[:, 2:3] * jnp.exp(st_ref[:, 0:1] - gst_ref[:, 0:1])
    emb_ref[...] = scale * (x_ref[...] - gst_ref[:, 1:2] * w_ref[...]) - SCALE * h


def final_pass(scalars, pieces, partner, x, w, st, gst):
    return pl.pallas_call(
        final_kernel,
        in_specs=[SMEM] + [VMEM] * 6,
        out_specs=[VMEM] * 2,
        out_shape=[jax.ShapeDtypeStruct((8, ROWS, D), BF16), jax.ShapeDtypeStruct((ROWS, D), F32)],
        name="final_pass",
    )(scalars, pieces, partner, x, w, st, gst)


CORE_PERM = [(i, i ^ 1) for i in range(DP)]
Y_PERM = [(i, i ^ 16) for i in range(DP)]
Z_GROUPS = [[y * 16 + z * 2 + c for z in range(8)] for y in range(2) for c in range(2)]


def exchange(x, axis, groups=None):
    return lax.all_to_all(x, axis, 0, 0, axis_index_groups=groups, tiled=True)


def swap(x, bit):
    return lax.ppermute(x, "proto", [(i, i ^ bit) for i in range(PR)])


def body(feature_matrix, tangent_embed, anchor_matrix, anchor_perturbation, codes, partner_lookup):
    dp = lax.axis_index("dp")
    q = lax.axis_index("proto")
    core = dp % 2
    y = dp // 16
    partner = partner_lookup.reshape(ROWS, 1)
    qs = q.reshape(1)

    block = mass_pass(qs, codes, tangent_embed)
    table = exchange(block, "dp")
    e, u, cst, st = score_pass(feature_matrix, tangent_embed, anchor_matrix, anchor_perturbation)
    h_part = h_pass(codes, anchor_perturbation)

    received = exchange(pick(qs, table, partner, st, h_part), "proto")
    x, w = embed_pass(e, u, anchor_matrix, anchor_perturbation, cst, st)
    f12, swt, gst, h_own = stats_pass(received, feature_matrix, tangent_embed, st, cst)

    mine_far, send_far = proto_pass(jnp.stack([core, 1 - y]), f12, swt, u, e, codes)
    got_far = lax.ppermute(send_far, "dp", CORE_PERM)
    h_pair = jnp.concatenate([h_own, lax.ppermute(h_own, "dp", CORE_PERM)], axis=0)
    to_y = (mine_far + got_far.astype(F32)).astype(BF16)
    from_far = lax.ppermute(to_y, "dp", Y_PERM)
    h_four = jnp.concatenate([h_pair, lax.ppermute(h_pair, "dp", Y_PERM)], axis=0)
    mine_near, send_near = proto_pass(jnp.stack([core, y]), f12, swt, u, e, codes)
    got_near = lax.ppermute(send_near, "dp", CORE_PERM)
    quarter = (mine_near + got_near.astype(F32) + from_far.astype(F32)).astype(BF16)
    quarter = jnp.concatenate([quarter, jnp.broadcast_to(h_four[None], (8, HR, D))], axis=1)
    pieces = exchange(quarter, "dp", Z_GROUPS)
    final, embed = final_pass(jnp.stack([q, core, y]), pieces, partner, x, w, st, gst)

    embed = embed + swap(embed, 4)
    along_z = exchange(final, "dp", Z_GROUPS)
    embed = embed + swap(embed, 2)
    from_y = lax.ppermute(along_z, "dp", Y_PERM)
    embed = embed + swap(embed, 1)
    own_core = lax.ppermute(along_z, "dp", CORE_PERM)
    far_core = lax.ppermute(from_y, "dp", CORE_PERM)
    own = jnp.where(core == 0, jnp.stack([along_z, own_core], 1), jnp.stack([own_core, along_z], 1))
    far = jnp.where(core == 0, jnp.stack([from_y, far_core], 1), jnp.stack([far_core, from_y], 1))
    hvp_proto = jnp.where(y == 0, jnp.stack([own, far]), jnp.stack([far, own])).reshape(LOCAL, D)
    return (embed.astype(BF16), hvp_proto)


def solution(mesh):
    in_specs = (
        P("dp", None),
        P("dp", None),
        P("proto", None),
        P("proto", None),
        P("dp", "proto"),
        P("dp"),
    )
    out_specs = (P("dp", None), P("proto", None))
    return jax.shard_map(body, mesh=mesh, in_specs=in_specs, out_specs=out_specs, check_vma=False)
```

```python
import jax
import jax.numpy as jnp
from jax import lax
from jax.experimental import pallas as pl
from jax.experimental.pallas import tpu as pltpu
from jax.sharding import PartitionSpec as P


F32 = jnp.float32
BF16 = jnp.bfloat16
NT = (((1,), (1,)), ((), ()))
TN = (((0,), (0,)), ((), ()))
D = 128
ROWS = 256
LOCAL = 8192
DP = 32
PR = 8
SUB = ROWS // PR
CN = 2048
NCH = LOCAL // CN
SCALE = 0.1
RG = 16
INV = 10.0
LOG2E = 1.4426950408889634
VMEM = pl.BlockSpec(memory_space=pltpu.VMEM)
SMEM = pl.BlockSpec(memory_space=pltpu.SMEM)
MB = 1024 * 1024


def split3(x):
    hi = x.astype(BF16).astype(F32)
    mid = (x - hi).astype(BF16).astype(F32)
    lo = (x - hi - mid).astype(BF16).astype(F32)
    return hi, mid, lo


def mass_kernel(q_ref, codes_ref, tan_ref, blk_ref, acc):
    step = pl.program_id(0)

    @pl.when(step == 0)
    def _():
        acc[...] = jnp.zeros_like(acc)

    for g in range(ROWS // RG):
        rows = slice(g * RG, (g + 1) * RG)
        x = codes_ref[rows, :].astype(F32)
        total = x[:, :D]
        for k in range(1, CN // D):
            total = total + x[:, k * D : (k + 1) * D]
        acc[rows, :] += total

    @pl.when(step == NCH - 1)
    def _():
        mass = jnp.sum(jnp.transpose(acc[...]), axis=0, keepdims=True)
        hi, mid, lo = split3(mass)
        parts = jnp.concatenate([hi, mid, lo, jnp.zeros((5, ROWS), F32)], axis=0)
        parts = jnp.concatenate([parts[:, :D], parts[:, D:]], axis=0).astype(BF16)
        rows = tan_ref[pl.ds(pl.multiple_of(q_ref[0] * SUB, SUB), SUB), :]
        block = jnp.concatenate([rows, parts], axis=0)
        for i in range(DP):
            blk_ref[i] = block


def mass_pass(q, codes, tan):
    return pl.pallas_call(
        mass_kernel,
        grid=(NCH,),
        in_specs=[
            SMEM,
            pl.BlockSpec((ROWS, CN), lambda c: (0, c)),
            pl.BlockSpec((ROWS, D), lambda c: (0, 0)),
        ],
        out_specs=pl.BlockSpec((DP, SUB + 16, D), lambda c: (0, 0, 0)),
        out_shape=jax.ShapeDtypeStruct((DP, SUB + 16, D), BF16),
        scratch_shapes=[pltpu.VMEM((ROWS, D), F32)],
        cost_estimate=pl.CostEstimate(flops=ROWS * LOCAL, bytes_accessed=5 << 20, transcendentals=0),
        compiler_params=pltpu.CompilerParams(vmem_limit_bytes=56 * MB),
        name="mass_pass",
    )(q, codes, tan)


def h_kernel(codes_ref, pert_ref, h_ref, acc):
    step = pl.program_id(0)

    @pl.when(step == 0)
    def _():
        acc[...] = jnp.zeros_like(acc)

    acc[...] += jnp.dot(codes_ref[...], pert_ref[...], preferred_element_type=F32)

    @pl.when(step == NCH - 1)
    def _():
        h_ref[...] = acc[...].astype(BF16)


def h_pass(codes, pert):
    return pl.pallas_call(
        h_kernel,
        grid=(NCH,),
        in_specs=[
            pl.BlockSpec((ROWS, CN), lambda c: (0, c)),
            pl.BlockSpec((CN, D), lambda c: (c, 0)),
        ],
        out_specs=pl.BlockSpec((ROWS, D), lambda c: (0, 0)),
        out_shape=jax.ShapeDtypeStruct((ROWS, D), BF16),
        scratch_shapes=[pltpu.VMEM((ROWS, D), F32)],
        cost_estimate=pl.CostEstimate(flops=2 * ROWS * LOCAL * D * 2, bytes_accessed=7 << 20, transcendentals=0),
        compiler_params=pltpu.CompilerParams(vmem_limit_bytes=56 * MB),
        name="h_pass",
    )(codes, pert)


def score_kernel(f_ref, tan_ref, a_ref, p_ref, e_ref, u_ref, cst_ref, st_ref, s_sc, t_sc, run):
    step = pl.program_id(0)
    f = f_ref[...]
    s_sc[...] = lax.dot_general(f, a_ref[...], NT, preferred_element_type=F32)
    left = jnp.concatenate([tan_ref[...], f], axis=1)
    right = jnp.concatenate([a_ref[...], p_ref[...]], axis=1)
    t_sc[...] = lax.dot_general(left, right, NT, preferred_element_type=F32)

    @pl.when(step == 0)
    def _():
        run[0] = jnp.full((ROWS, D), -jnp.inf, F32)
        run[1] = jnp.zeros((ROWS, D), F32)
        run[2] = jnp.zeros((ROWS, D), F32)

    lane = lax.broadcasted_iota(jnp.int32, (RG, D), 1)
    for g in range(ROWS // RG):
        rows = slice(g * RG, (g + 1) * RG)
        s = s_sc[rows, :]
        t = t_sc[rows, :]
        top = jnp.max(s, axis=1, keepdims=True)
        e = jnp.exp2((s - top) * (INV * LOG2E))
        z = jnp.sum(e, axis=1, keepdims=True)
        et = jnp.sum(e * t, axis=1, keepdims=True)
        mean = et / z
        e_ref[rows, :] = e.astype(BF16)
        u_ref[rows, :] = (e * (t - mean)).astype(BF16)
        top = top * INV
        cst_ref[0, rows, :] = jnp.where(lane == 0, top, mean * INV)
        old = run[0, rows, :]
        new = jnp.maximum(old, top)
        alpha = jnp.exp(old - new)
        beta = jnp.exp(top - new)
        z_run = run[1, rows, :] * alpha + beta * z
        et_run = run[2, rows, :] * alpha + beta * (et * INV)
        run[0, rows, :] = new
        run[1, rows, :] = z_run
        run[2, rows, :] = et_run
        st_ref[rows, :] = jnp.where(lane == 0, new, jnp.where(lane == 1, z_run, et_run))


def score_pass(f, tan, a, p):
    return pl.pallas_call(
        score_kernel,
        grid=(NCH,),
        in_specs=[
            pl.BlockSpec((ROWS, D), lambda c: (0, 0)),
            pl.BlockSpec((ROWS, D), lambda c: (0, 0)),
            pl.BlockSpec((CN, D), lambda c: (c, 0)),
            pl.BlockSpec((CN, D), lambda c: (c, 0)),
        ],
        out_specs=[
            pl.BlockSpec((ROWS, CN), lambda c: (0, c)),
            pl.BlockSpec((ROWS, CN), lambda c: (0, c)),
            pl.BlockSpec((1, ROWS, D), lambda c: (c, 0, 0)),
            pl.BlockSpec((ROWS, D), lambda c: (0, 0)),
        ],
        out_shape=[
            jax.ShapeDtypeStruct((ROWS, LOCAL), BF16),
            jax.ShapeDtypeStruct((ROWS, LOCAL), BF16),
            jax.ShapeDtypeStruct((NCH, ROWS, D), F32),
            jax.ShapeDtypeStruct((ROWS, D), F32),
        ],
        scratch_shapes=[
            pltpu.VMEM((ROWS, CN), F32),
            pltpu.VMEM((ROWS, CN), F32),
            pltpu.VMEM((3, ROWS, D), F32),
        ],
        cost_estimate=pl.CostEstimate(flops=10 * ROWS * LOCAL * D * 2, bytes_accessed=12 << 20, transcendentals=ROWS * LOCAL),
        compiler_params=pltpu.CompilerParams(vmem_limit_bytes=56 * MB),
        name="score_pass",
    )(f, tan, a, p)


def embed_kernel(e_ref, u_ref, a_ref, p_ref, cst_ref, st_ref, x_ref, w_ref):
    @pl.when(pl.program_id(0) == 0)
    def _():
        x_ref[...] = jnp.zeros_like(x_ref)
        w_ref[...] = jnp.zeros_like(w_ref)

    e = e_ref[...]
    both = jnp.dot(e, jnp.concatenate([a_ref[...], p_ref[...]], axis=1), preferred_element_type=F32)
    ua = jnp.dot(u_ref[...], a_ref[...], preferred_element_type=F32)
    ea = both[:, :D]
    beta = jnp.exp(cst_ref[0, :, 0:1] - st_ref[:, 0:1])
    mean = cst_ref[0, :, 1:2]
    x_ref[...] += beta * (INV * ua + both[:, D:] + mean * ea)
    w_ref[...] += beta * ea


def embed_pass(e, u, a, p, cst, st):
    return pl.pallas_call(
        embed_kernel,
        grid=(NCH,),
        in_specs=[
            pl.BlockSpec((ROWS, CN), lambda c: (0, c)),
            pl.BlockSpec((ROWS, CN), lambda c: (0, c)),
            pl.BlockSpec((CN, D), lambda c: (c, 0)),
            pl.BlockSpec((CN, D), lambda c: (c, 0)),
            pl.BlockSpec((1, ROWS, D), lambda c: (c, 0, 0)),
            pl.BlockSpec((ROWS, D), lambda c: (0, 0)),
        ],
        out_specs=[
            pl.BlockSpec((ROWS, D), lambda c: (0, 0)),
            pl.BlockSpec((ROWS, D), lambda c: (0, 0)),
        ],
        out_shape=[jax.ShapeDtypeStruct((ROWS, D), F32)] * 2,
        cost_estimate=pl.CostEstimate(flops=6 * ROWS * LOCAL * D * 2, bytes_accessed=12 << 20, transcendentals=0),
        compiler_params=pltpu.CompilerParams(vmem_limit_bytes=56 * MB),
        name="embed_pass",
    )(e, u, a, p, cst, st)


STAT = 16
PAY = ROWS + 2 * STAT + SUB


def pick_kernel(q_ref, tab_ref, part_ref, st_ref, h_ref, pay_ref):
    q = q_ref[0]
    partner = part_ref[...]
    group = partner // ROWS
    row = partner % ROWS
    mine = (row // SUB) == q
    column = jnp.where(mine, group * SUB + row % SUB, -1)
    hot = (lax.broadcasted_iota(jnp.int32, (ROWS, DP * SUB), 1) == column).astype(F32).astype(BF16)
    table = tab_ref[:, :SUB, :].reshape(DP * SUB, D)
    rows = jnp.dot(hot, table, preferred_element_type=F32).astype(BF16)

    hot_group = (lax.broadcasted_iota(jnp.int32, (ROWS, DP), 1) == group).astype(F32).astype(BF16)
    mass_rows = tab_ref[:, SUB:, :].astype(F32)
    mass = jnp.zeros((ROWS, ROWS), F32)
    for k in (2, 1, 0):
        piece = jnp.concatenate([mass_rows[:, k, :], mass_rows[:, 8 + k, :]], axis=1).astype(BF16)
        mass = mass + jnp.dot(hot_group, piece, preferred_element_type=F32)
    here = lax.broadcasted_iota(jnp.int32, (ROWS, ROWS), 1) == row
    mass = jnp.sum(jnp.where(here, mass, 0.0), axis=1, keepdims=True)

    lane = lax.broadcasted_iota(jnp.int32, (ROWS, D), 1)
    stats = jnp.where(lane == 3, mass, st_ref[...])
    flat = jnp.transpose(stats)[:4, :]
    hi, mid, lo = split3(flat)
    flat = jnp.concatenate([hi, mid, lo, jnp.zeros((STAT - 12, ROWS), F32)], axis=0)
    flat = jnp.concatenate([flat[:, :D], flat[:, D:]], axis=0).astype(BF16)
    payload = jnp.concatenate([rows, flat], axis=0)
    for i in range(PR):
        pay_ref[i, : ROWS + 2 * STAT, :] = payload
        pay_ref[i, ROWS + 2 * STAT :, :] = h_ref[i * SUB : (i + 1) * SUB, :]


def pick(q, tab, partner, st, h):
    return pl.pallas_call(
        pick_kernel,
        in_specs=[SMEM, VMEM, VMEM, VMEM, VMEM],
        out_specs=VMEM,
        out_shape=jax.ShapeDtypeStruct((PR, PAY, D), BF16),
        compiler_params=pltpu.CompilerParams(vmem_limit_bytes=10 * MB),
        name="pick",
    )(q, tab, partner, st, h)


def stats_kernel(rec_ref, f_ref, tan_ref, st_ref, cst_ref, f12_ref, swt_ref, gst_ref, h_ref):
    total = jnp.zeros((ROWS, D), F32)
    h = jnp.zeros((SUB, D), F32)
    flats = []
    for i in range(PR):
        total = total + rec_ref[i, :ROWS, :].astype(F32)
        flat = rec_ref[i, ROWS : ROWS + 2 * STAT, :].astype(F32)
        flat = jnp.concatenate([flat[:STAT], flat[STAT:]], axis=1)
        flats.append((flat[0:4] + flat[4:8]) + flat[8:12])
        h = h + rec_ref[i, ROWS + 2 * STAT :, :].astype(F32)
    swt_ref[...] = (total * SCALE).astype(BF16)
    h_ref[...] = h.astype(BF16)
    top = flats[0][0:1]
    for i in range(1, PR):
        top = jnp.maximum(top, flats[i][0:1])
    z = jnp.zeros((1, ROWS), F32)
    et = jnp.zeros((1, ROWS), F32)
    mass = jnp.zeros((1, ROWS), F32)
    for i in range(PR):
        shift = jnp.exp(flats[i][0:1] - top)
        z = z + shift * flats[i][1:2]
        et = et + shift * flats[i][2:3]
        mass = mass + flats[i][3:4]
    rows = jnp.concatenate([top, et / z, SCALE * mass / z, jnp.zeros((D - 3, ROWS), F32)], axis=0)
    cols = jnp.transpose(rows)
    gst_ref[...] = cols
    top = cols[:, 0:1]
    mean = cols[:, 1:2]
    weight = cols[:, 2:3]
    f = f_ref[...].astype(F32)
    tan = tan_ref[...].astype(F32)
    for c in range(NCH):
        scale = weight * jnp.exp(cst_ref[c, :, 0:1] - top)
        f12_ref[c, :, :D] = (INV * scale * f).astype(BF16)
        f12_ref[c, :, D:] = (scale * ((cst_ref[c, :, 1:2] - mean) * f + tan)).astype(BF16)


def stats_pass(rec, f, tan, st, cst):
    return pl.pallas_call(
        stats_kernel,
        in_specs=[VMEM] * 5,
        out_specs=[VMEM] * 4,
        out_shape=[
            jax.ShapeDtypeStruct((NCH, ROWS, 2 * D), BF16),
            jax.ShapeDtypeStruct((ROWS, D), BF16),
            jax.ShapeDtypeStruct((ROWS, D), F32),
            jax.ShapeDtypeStruct((SUB, D), BF16),
        ],
        compiler_params=pltpu.CompilerParams(vmem_limit_bytes=10 * MB),
        name="stats_pass",
    )(rec, f, tan, st, cst)


def proto_kernel(s_ref, f12_ref, swt_ref, u_ref, e_ref, codes_ref, mine_ref, send_ref):
    f12 = f12_ref[0]
    res = lax.dot_general(u_ref[...], f12[:, :D], TN, preferred_element_type=F32)
    res = res + lax.dot_general(e_ref[...], f12[:, D:], TN, preferred_element_type=F32)
    res = res - lax.dot_general(codes_ref[...], swt_ref[...], TN, preferred_element_type=F32)
    first = s_ref[0] == 0
    for b in range(CN // (2 * ROWS)):
        even = res[2 * b * ROWS : (2 * b + 1) * ROWS]
        odd = res[(2 * b + 1) * ROWS : (2 * b + 2) * ROWS]
        mine_ref[b] = jnp.where(first, even, odd)
        send_ref[b] = jnp.where(first, odd, even).astype(BF16)


def proto_pass(scalars, f12, swt, u, e, codes):
    nb = CN // (2 * ROWS)
    steps = NCH // 2
    wide = pl.BlockSpec((ROWS, CN), lambda c, s: (0, s[1] * steps + c))
    return pl.pallas_call(
        proto_kernel,
        grid_spec=pltpu.PrefetchScalarGridSpec(
            num_scalar_prefetch=1,
            grid=(steps,),
            in_specs=[
                pl.BlockSpec((1, ROWS, 2 * D), lambda c, s: (s[1] * steps + c, 0, 0)),
                pl.BlockSpec((ROWS, D), lambda c, s: (0, 0)),
                wide,
                wide,
                wide,
            ],
            out_specs=[
                pl.BlockSpec((nb, ROWS, D), lambda c, s: (c, 0, 0)),
                pl.BlockSpec((nb, ROWS, D), lambda c, s: (c, 0, 0)),
            ],
        ),
        out_shape=[
            jax.ShapeDtypeStruct((8, ROWS, D), F32),
            jax.ShapeDtypeStruct((8, ROWS, D), BF16),
        ],
        cost_estimate=pl.CostEstimate(flops=3 * ROWS * LOCAL * D * 2, bytes_accessed=9 << 20, transcendentals=0),
        compiler_params=pltpu.CompilerParams(vmem_limit_bytes=56 * MB),
        name="proto_pass",
    )(scalars, f12, swt, u, e, codes)


HR = 2 * SUB


def final_kernel(pieces_ref, out_ref):
    total = pieces_ref[0].astype(F32)
    for i in range(1, 8):
        total = total + pieces_ref[i].astype(F32)
    total = total.astype(BF16)
    for i in range(8):
        out_ref[i] = total


def final_pass(pieces):
    return pl.pallas_call(
        final_kernel,
        in_specs=[VMEM],
        out_specs=VMEM,
        out_shape=jax.ShapeDtypeStruct((8, ROWS, D), BF16),
        compiler_params=pltpu.CompilerParams(vmem_limit_bytes=8 * MB),
        name="final_pass",
    )(pieces)


def row_kernel(s_ref, near_ref, far_ref, part_ref, x_ref, w_ref, st_ref, gst_ref, emb_ref):
    q = s_ref[0]
    core = s_ref[1]
    y = s_ref[2]
    partner = part_ref[...]
    group = partner // ROWS
    row = partner % ROWS
    c_rel = jnp.where(group % 2 == core, 0, 1)
    column = ((group // 2) % 8) * HR + c_rel * SUB + row % SUB
    mine = (row // SUB) == q
    h = jnp.zeros((ROWS, D), F32)
    for table_ref, side in ((near_ref, y), (far_ref, 1 - y)):
        col = jnp.where(jnp.logical_and(mine, group // 16 == side), column, -1)
        hot = (lax.broadcasted_iota(jnp.int32, (ROWS, 8 * HR), 1) == col).astype(F32).astype(BF16)
        h = h + jnp.dot(hot, table_ref[...].reshape(8 * HR, D), preferred_element_type=F32)
    scale = gst_ref[:, 2:3] * jnp.exp(st_ref[:, 0:1] - gst_ref[:, 0:1])
    emb_ref[...] = scale * (x_ref[...] - gst_ref[:, 1:2] * w_ref[...]) - SCALE * h


def row_pass(scalars, near, far, partner, x, w, st, gst):
    return pl.pallas_call(
        row_kernel,
        in_specs=[SMEM] + [VMEM] * 7,
        out_specs=VMEM,
        out_shape=jax.ShapeDtypeStruct((ROWS, D), F32),
        compiler_params=pltpu.CompilerParams(vmem_limit_bytes=8 * MB),
        name="row_pass",
    )(scalars, near, far, partner, x, w, st, gst)


CORE_PERM = [(i, i ^ 1) for i in range(DP)]
Y_PERM = [(i, i ^ 16) for i in range(DP)]
Z_GROUPS = [[y * 16 + z * 2 + c for z in range(8)] for y in range(2) for c in range(2)]


def exchange(x, axis, groups=None):
    return lax.all_to_all(x, axis, 0, 0, axis_index_groups=groups, tiled=True)


def swap(x, bit):
    return lax.ppermute(x, "proto", [(i, i ^ bit) for i in range(PR)])


def inner(feature_matrix, tangent_embed, anchor_matrix, anchor_perturbation, codes, partner_lookup):
    dp = lax.axis_index("dp")
    q = lax.axis_index("proto")
    core = dp % 2
    y = dp // 16
    partner = partner_lookup.reshape(ROWS, 1)
    qs = q.reshape(1)

    block = mass_pass(qs, codes, tangent_embed)
    table = exchange(block, "dp")
    e, u, cst, st = score_pass(feature_matrix, tangent_embed, anchor_matrix, anchor_perturbation)
    h_part = h_pass(codes, anchor_perturbation)

    received = exchange(pick(qs, table, partner, st, h_part), "proto")
    x, w = embed_pass(e, u, anchor_matrix, anchor_perturbation, cst, st)
    received, x, w = lax.optimization_barrier((received, x, w))
    f12, swt, gst, h_own = stats_pass(received, feature_matrix, tangent_embed, st, cst)

    mine_far, send_far = proto_pass(jnp.stack([core, 1 - y]), f12, swt, u, e, codes)
    got_far = lax.ppermute(send_far, "dp", CORE_PERM)
    h_pair = jnp.concatenate([h_own, lax.ppermute(h_own, "dp", CORE_PERM)], axis=0)
    to_y = (mine_far + got_far.astype(F32)).astype(BF16)
    from_far = lax.ppermute(to_y, "dp", Y_PERM)
    f12, swt, to_y = lax.optimization_barrier((f12, swt, to_y))
    mine_near, send_near = proto_pass(jnp.stack([core, y]), f12, swt, u, e, codes)
    got_near = lax.ppermute(send_near, "dp", CORE_PERM)
    h_pair, mine_near = lax.optimization_barrier((h_pair, mine_near))
    h_near = exchange(jnp.broadcast_to(h_pair[None], (8, HR, D)), "dp", Z_GROUPS)
    quarter = (mine_near + got_near.astype(F32) + from_far.astype(F32)).astype(BF16)
    quarter, h_near = lax.optimization_barrier((quarter, h_near))
    h_far = lax.ppermute(h_near, "dp", Y_PERM)
    pieces = exchange(quarter, "dp", Z_GROUPS)
    embed = row_pass(jnp.stack([q, core, y]), h_near, h_far, partner, x, w, st, gst)
    embed = embed + swap(embed, 4)
    pieces, embed = lax.optimization_barrier((pieces, embed))
    final = final_pass(pieces)

    swapped = swap(embed, 2)
    along_z = exchange(final, "dp", Z_GROUPS)
    from_y = lax.ppermute(along_z, "dp", Y_PERM)
    embed = embed + swapped
    embed = embed + swap(embed, 1)
    own_core = lax.ppermute(along_z, "dp", CORE_PERM)
    far_core = lax.ppermute(from_y, "dp", CORE_PERM)
    own = jnp.where(core == 0, jnp.stack([along_z, own_core], 1), jnp.stack([own_core, along_z], 1))
    far = jnp.where(core == 0, jnp.stack([from_y, far_core], 1), jnp.stack([far_core, from_y], 1))
    hvp_proto = jnp.where(y == 0, jnp.stack([own, far]), jnp.stack([far, own])).reshape(LOCAL, D)
    return (embed.astype(BF16), hvp_proto)


def solution(mesh):
    in_specs = (
        P("dp", None),
        P("dp", None),
        P("proto", None),
        P("proto", None),
        P("dp", "proto"),
        P("dp"),
    )
    out_specs = (P("dp", None), P("proto", None))
    return jax.shard_map(inner, mesh=mesh, in_specs=in_specs, out_specs=out_specs, check_vma=False)
```

```python
import jax
import jax.numpy as jnp
from jax import lax
from jax.experimental import pallas as pl
from jax.experimental.pallas import tpu as pltpu
from jax.sharding import PartitionSpec as P


F32 = jnp.float32
BF16 = jnp.bfloat16
NT = (((1,), (1,)), ((), ()))
TN = (((0,), (0,)), ((), ()))
D = 128
ROWS = 256
LOCAL = 8192
DP = 32
PR = 8
SUB = ROWS // PR
CN = 2048
NCH = LOCAL // CN
SCALE = 0.1
RG = 16
INV = 10.0
LOG2E = 1.4426950408889634
VMEM = pl.BlockSpec(memory_space=pltpu.VMEM)
SMEM = pl.BlockSpec(memory_space=pltpu.SMEM)
MB = 1024 * 1024


def split3(x):
    hi = x.astype(BF16).astype(F32)
    mid = (x - hi).astype(BF16).astype(F32)
    lo = (x - hi - mid).astype(BF16).astype(F32)
    return hi, mid, lo


def mass_kernel(q_ref, codes_ref, tan_ref, blk_ref, acc):
    step = pl.program_id(0)

    @pl.when(step == 0)
    def _():
        acc[...] = jnp.zeros_like(acc)

    for g in range(ROWS // RG):
        rows = slice(g * RG, (g + 1) * RG)
        x = codes_ref[rows, :].astype(F32)
        total = x[:, :D]
        for k in range(1, CN // D):
            total = total + x[:, k * D : (k + 1) * D]
        acc[rows, :] += total

    @pl.when(step == NCH - 1)
    def _():
        mass = jnp.sum(jnp.transpose(acc[...]), axis=0, keepdims=True)
        hi, mid, lo = split3(mass)
        parts = jnp.concatenate([hi, mid, lo, jnp.zeros((5, ROWS), F32)], axis=0)
        parts = jnp.concatenate([parts[:, :D], parts[:, D:]], axis=0).astype(BF16)
        rows = tan_ref[pl.ds(pl.multiple_of(q_ref[0] * SUB, SUB), SUB), :]
        block = jnp.concatenate([rows, parts], axis=0)
        for i in range(DP):
            blk_ref[i] = block


def mass_pass(q, codes, tan):
    return pl.pallas_call(
        mass_kernel,
        grid=(NCH,),
        in_specs=[
            SMEM,
            pl.BlockSpec((ROWS, CN), lambda c: (0, c)),
            pl.BlockSpec((ROWS, D), lambda c: (0, 0)),
        ],
        out_specs=pl.BlockSpec((DP, SUB + 16, D), lambda c: (0, 0, 0)),
        out_shape=jax.ShapeDtypeStruct((DP, SUB + 16, D), BF16),
        scratch_shapes=[pltpu.VMEM((ROWS, D), F32)],
        cost_estimate=pl.CostEstimate(flops=ROWS * LOCAL, bytes_accessed=5 << 20, transcendentals=0),
        compiler_params=pltpu.CompilerParams(vmem_limit_bytes=56 * MB),
        name="mass_pass",
    )(q, codes, tan)


def score_kernel(f_ref, tan_ref, a_ref, p_ref, codes_ref, e_ref, u_ref, cst_ref, st_ref, h_ref, s_sc, t_sc, run, acc):
    step = pl.program_id(0)
    f = f_ref[...]
    s_sc[...] = lax.dot_general(f, a_ref[...], NT, preferred_element_type=F32)
    left = jnp.concatenate([tan_ref[...], f], axis=1)
    right = jnp.concatenate([a_ref[...], p_ref[...]], axis=1)
    t_sc[...] = lax.dot_general(left, right, NT, preferred_element_type=F32)

    @pl.when(step == 0)
    def _():
        run[0] = jnp.full((ROWS, D), -jnp.inf, F32)
        run[1] = jnp.zeros((ROWS, D), F32)
        run[2] = jnp.zeros((ROWS, D), F32)
        acc[...] = jnp.zeros_like(acc)

    acc[...] += jnp.dot(codes_ref[...], p_ref[...], preferred_element_type=F32)
    h_ref[...] = acc[...].astype(BF16)
    lane = lax.broadcasted_iota(jnp.int32, (RG, D), 1)
    for g in range(ROWS // RG):
        rows = slice(g * RG, (g + 1) * RG)
        s = s_sc[rows, :]
        t = t_sc[rows, :]
        top = jnp.max(s, axis=1, keepdims=True)
        e = jnp.exp2((s - top) * (INV * LOG2E))
        z = jnp.sum(e, axis=1, keepdims=True)
        et = jnp.sum(e * t, axis=1, keepdims=True)
        mean = et / z
        e_ref[rows, :] = e.astype(BF16)
        u_ref[rows, :] = (e * (t - mean)).astype(BF16)
        top = top * INV
        cst_ref[0, rows, :] = jnp.where(lane == 0, top, mean * INV)
        old = run[0, rows, :]
        new = jnp.maximum(old, top)
        alpha = jnp.exp(old - new)
        beta = jnp.exp(top - new)
        z_run = run[1, rows, :] * alpha + beta * z
        et_run = run[2, rows, :] * alpha + beta * (et * INV)
        run[0, rows, :] = new
        run[1, rows, :] = z_run
        run[2, rows, :] = et_run
        st_ref[rows, :] = jnp.where(lane == 0, new, jnp.where(lane == 1, z_run, et_run))


def score_pass(f, tan, a, p, codes):
    return pl.pallas_call(
        score_kernel,
        grid=(NCH,),
        in_specs=[
            pl.BlockSpec((ROWS, D), lambda c: (0, 0)),
            pl.BlockSpec((ROWS, D), lambda c: (0, 0)),
            pl.BlockSpec((CN, D), lambda c: (c, 0)),
            pl.BlockSpec((CN, D), lambda c: (c, 0)),
            pl.BlockSpec((ROWS, CN), lambda c: (0, c)),
        ],
        out_specs=[
            pl.BlockSpec((ROWS, CN), lambda c: (0, c)),
            pl.BlockSpec((ROWS, CN), lambda c: (0, c)),
            pl.BlockSpec((1, ROWS, D), lambda c: (c, 0, 0)),
            pl.BlockSpec((ROWS, D), lambda c: (0, 0)),
            pl.BlockSpec((ROWS, D), lambda c: (0, 0)),
        ],
        out_shape=[
            jax.ShapeDtypeStruct((ROWS, LOCAL), BF16),
            jax.ShapeDtypeStruct((ROWS, LOCAL), BF16),
            jax.ShapeDtypeStruct((NCH, ROWS, D), F32),
            jax.ShapeDtypeStruct((ROWS, D), F32),
            jax.ShapeDtypeStruct((ROWS, D), BF16),
        ],
        scratch_shapes=[
            pltpu.VMEM((ROWS, CN), F32),
            pltpu.VMEM((ROWS, CN), F32),
            pltpu.VMEM((3, ROWS, D), F32),
            pltpu.VMEM((ROWS, D), F32),
        ],
        cost_estimate=pl.CostEstimate(flops=10 * ROWS * LOCAL * D * 2, bytes_accessed=12 << 20, transcendentals=ROWS * LOCAL),
        compiler_params=pltpu.CompilerParams(vmem_limit_bytes=56 * MB),
        name="score_pass",
    )(f, tan, a, p, codes)


def embed_kernel(e_ref, u_ref, a_ref, p_ref, cst_ref, st_ref, x_ref, w_ref):
    @pl.when(pl.program_id(0) == 0)
    def _():
        x_ref[...] = jnp.zeros_like(x_ref)
        w_ref[...] = jnp.zeros_like(w_ref)

    e = e_ref[...]
    both = jnp.dot(e, jnp.concatenate([a_ref[...], p_ref[...]], axis=1), preferred_element_type=F32)
    ua = jnp.dot(u_ref[...], a_ref[...], preferred_element_type=F32)
    ea = both[:, :D]
    beta = jnp.exp(cst_ref[0, :, 0:1] - st_ref[:, 0:1])
    mean = cst_ref[0, :, 1:2]
    x_ref[...] += beta * (INV * ua + both[:, D:] + mean * ea)
    w_ref[...] += beta * ea


def embed_pass(e, u, a, p, cst, st):
    return pl.pallas_call(
        embed_kernel,
        grid=(NCH,),
        in_specs=[
            pl.BlockSpec((ROWS, CN), lambda c: (0, c)),
            pl.BlockSpec((ROWS, CN), lambda c: (0, c)),
            pl.BlockSpec((CN, D), lambda c: (c, 0)),
            pl.BlockSpec((CN, D), lambda c: (c, 0)),
            pl.BlockSpec((1, ROWS, D), lambda c: (c, 0, 0)),
            pl.BlockSpec((ROWS, D), lambda c: (0, 0)),
        ],
        out_specs=[
            pl.BlockSpec((ROWS, D), lambda c: (0, 0)),
            pl.BlockSpec((ROWS, D), lambda c: (0, 0)),
        ],
        out_shape=[jax.ShapeDtypeStruct((ROWS, D), F32)] * 2,
        cost_estimate=pl.CostEstimate(flops=6 * ROWS * LOCAL * D * 2, bytes_accessed=12 << 20, transcendentals=0),
        compiler_params=pltpu.CompilerParams(vmem_limit_bytes=56 * MB),
        name="embed_pass",
    )(e, u, a, p, cst, st)


STAT = 16
PAY = ROWS + 2 * STAT + SUB


def pick_kernel(q_ref, tab_ref, part_ref, st_ref, h_ref, pay_ref):
    q = q_ref[0]
    partner = part_ref[...]
    group = partner // ROWS
    row = partner % ROWS
    mine = (row // SUB) == q
    column = jnp.where(mine, group * SUB + row % SUB, -1)
    hot = (lax.broadcasted_iota(jnp.int32, (ROWS, DP * SUB), 1) == column).astype(F32).astype(BF16)
    table = tab_ref[:, :SUB, :].reshape(DP * SUB, D)
    rows = jnp.dot(hot, table, preferred_element_type=F32).astype(BF16)

    hot_group = (lax.broadcasted_iota(jnp.int32, (ROWS, DP), 1) == group).astype(F32).astype(BF16)
    mass_rows = tab_ref[:, SUB:, :].astype(F32)
    mass = jnp.zeros((ROWS, ROWS), F32)
    for k in (2, 1, 0):
        piece = jnp.concatenate([mass_rows[:, k, :], mass_rows[:, 8 + k, :]], axis=1).astype(BF16)
        mass = mass + jnp.dot(hot_group, piece, preferred_element_type=F32)
    here = lax.broadcasted_iota(jnp.int32, (ROWS, ROWS), 1) == row
    mass = jnp.sum(jnp.where(here, mass, 0.0), axis=1, keepdims=True)

    lane = lax.broadcasted_iota(jnp.int32, (ROWS, D), 1)
    stats = jnp.where(lane == 3, mass, st_ref[...])
    flat = jnp.transpose(stats)[:4, :]
    hi, mid, lo = split3(flat)
    flat = jnp.concatenate([hi, mid, lo, jnp.zeros((STAT - 12, ROWS), F32)], axis=0)
    flat = jnp.concatenate([flat[:, :D], flat[:, D:]], axis=0).astype(BF16)
    payload = jnp.concatenate([rows, flat], axis=0)
    for i in range(PR):
        pay_ref[i, : ROWS + 2 * STAT, :] = payload
        pay_ref[i, ROWS + 2 * STAT :, :] = h_ref[i * SUB : (i + 1) * SUB, :]


def pick(q, tab, partner, st, h):
    return pl.pallas_call(
        pick_kernel,
        in_specs=[SMEM, VMEM, VMEM, VMEM, VMEM],
        out_specs=VMEM,
        out_shape=jax.ShapeDtypeStruct((PR, PAY, D), BF16),
        compiler_params=pltpu.CompilerParams(vmem_limit_bytes=10 * MB),
        name="pick",
    )(q, tab, partner, st, h)


def stats_kernel(rec_ref, f_ref, tan_ref, st_ref, cst_ref, f12_ref, swt_ref, gst_ref, h_ref):
    total = jnp.zeros((ROWS, D), F32)
    h = jnp.zeros((SUB, D), F32)
    flats = []
    for i in range(PR):
        total = total + rec_ref[i, :ROWS, :].astype(F32)
        flat = rec_ref[i, ROWS : ROWS + 2 * STAT, :].astype(F32)
        flat = jnp.concatenate([flat[:STAT], flat[STAT:]], axis=1)
        flats.append((flat[0:4] + flat[4:8]) + flat[8:12])
        h = h + rec_ref[i, ROWS + 2 * STAT :, :].astype(F32)
    swt_ref[...] = (total * SCALE).astype(BF16)
    h_ref[...] = h.astype(BF16)
    top = flats[0][0:1]
    for i in range(1, PR):
        top = jnp.maximum(top, flats[i][0:1])
    z = jnp.zeros((1, ROWS), F32)
    et = jnp.zeros((1, ROWS), F32)
    mass = jnp.zeros((1, ROWS), F32)
    for i in range(PR):
        shift = jnp.exp(flats[i][0:1] - top)
        z = z + shift * flats[i][1:2]
        et = et + shift * flats[i][2:3]
        mass = mass + flats[i][3:4]
    rows = jnp.concatenate([top, et / z, SCALE * mass / z, jnp.zeros((D - 3, ROWS), F32)], axis=0)
    cols = jnp.transpose(rows)
    gst_ref[...] = cols
    top = cols[:, 0:1]
    mean = cols[:, 1:2]
    weight = cols[:, 2:3]
    f = f_ref[...].astype(F32)
    tan = tan_ref[...].astype(F32)
    for c in range(NCH):
        scale = weight * jnp.exp(cst_ref[c, :, 0:1] - top)
        f12_ref[c, :, :D] = (INV * scale * f).astype(BF16)
        f12_ref[c, :, D:] = (scale * ((cst_ref[c, :, 1:2] - mean) * f + tan)).astype(BF16)


def stats_pass(rec, f, tan, st, cst):
    return pl.pallas_call(
        stats_kernel,
        in_specs=[VMEM] * 5,
        out_specs=[VMEM] * 4,
        out_shape=[
            jax.ShapeDtypeStruct((NCH, ROWS, 2 * D), BF16),
            jax.ShapeDtypeStruct((ROWS, D), BF16),
            jax.ShapeDtypeStruct((ROWS, D), F32),
            jax.ShapeDtypeStruct((SUB, D), BF16),
        ],
        compiler_params=pltpu.CompilerParams(vmem_limit_bytes=10 * MB),
        name="stats_pass",
    )(rec, f, tan, st, cst)


def proto_kernel(s_ref, f12_ref, swt_ref, u_ref, e_ref, codes_ref, mine_ref, send_ref):
    f12 = f12_ref[0]
    res = lax.dot_general(u_ref[...], f12[:, :D], TN, preferred_element_type=F32)
    res = res + lax.dot_general(e_ref[...], f12[:, D:], TN, preferred_element_type=F32)
    res = res - lax.dot_general(codes_ref[...], swt_ref[...], TN, preferred_element_type=F32)
    first = s_ref[0] == 0
    for b in range(CN // (2 * ROWS)):
        even = res[2 * b * ROWS : (2 * b + 1) * ROWS]
        odd = res[(2 * b + 1) * ROWS : (2 * b + 2) * ROWS]
        mine_ref[b] = jnp.where(first, even, odd)
        send_ref[b] = jnp.where(first, odd, even).astype(BF16)


def proto_pass(scalars, f12, swt, u, e, codes):
    nb = CN // (2 * ROWS)
    steps = NCH // 2
    wide = pl.BlockSpec((ROWS, CN), lambda c, s: (0, s[1] * steps + c))
    return pl.pallas_call(
        proto_kernel,
        grid_spec=pltpu.PrefetchScalarGridSpec(
            num_scalar_prefetch=1,
            grid=(steps,),
            in_specs=[
                pl.BlockSpec((1, ROWS, 2 * D), lambda c, s: (s[1] * steps + c, 0, 0)),
                pl.BlockSpec((ROWS, D), lambda c, s: (0, 0)),
                wide,
                wide,
                wide,
            ],
            out_specs=[
                pl.BlockSpec((nb, ROWS, D), lambda c, s: (c, 0, 0)),
                pl.BlockSpec((nb, ROWS, D), lambda c, s: (c, 0, 0)),
            ],
        ),
        out_shape=[
            jax.ShapeDtypeStruct((8, ROWS, D), F32),
            jax.ShapeDtypeStruct((8, ROWS, D), BF16),
        ],
        cost_estimate=pl.CostEstimate(flops=3 * ROWS * LOCAL * D * 2, bytes_accessed=9 << 20, transcendentals=0),
        compiler_params=pltpu.CompilerParams(vmem_limit_bytes=56 * MB),
        name="proto_pass",
    )(scalars, f12, swt, u, e, codes)


def final_kernel(pieces_ref, out_ref):
    total = pieces_ref[0].astype(F32)
    for i in range(1, 8):
        total = total + pieces_ref[i].astype(F32)
    total = total.astype(BF16)
    for i in range(8):
        out_ref[i] = total


def final_pass(pieces):
    return pl.pallas_call(
        final_kernel,
        in_specs=[VMEM],
        out_specs=VMEM,
        out_shape=jax.ShapeDtypeStruct((8, ROWS, D), BF16),
        compiler_params=pltpu.CompilerParams(vmem_limit_bytes=8 * MB),
        name="final_pass",
    )(pieces)


def row_kernel(s_ref, own_ref, other_ref, part_ref, x_ref, w_ref, st_ref, gst_ref, emb_ref):
    q = s_ref[0]
    partner = part_ref[...]
    away = (partner // ROWS) ^ s_ref[1]
    block = ((away >> 3) & 1) + 2 * ((away >> 2) & 1) + 4 * ((away >> 1) & 1) + 8 * ((away >> 4) & 1) + 16 * (away & 1)
    row = partner % ROWS
    column = jnp.where((row // SUB) == q, block * SUB + row % SUB, -1)
    hot = (lax.broadcasted_iota(jnp.int32, (ROWS, DP * SUB), 1) == column).astype(F32).astype(BF16)
    table = jnp.concatenate([own_ref[...], other_ref[...]], axis=0)
    h = jnp.dot(hot, table, preferred_element_type=F32)
    scale = gst_ref[:, 2:3] * jnp.exp(st_ref[:, 0:1] - gst_ref[:, 0:1])
    emb_ref[...] = scale * (x_ref[...] - gst_ref[:, 1:2] * w_ref[...]) - SCALE * h


def row_pass(scalars, own, other, partner, x, w, st, gst):
    return pl.pallas_call(
        row_kernel,
        in_specs=[SMEM] + [VMEM] * 7,
        out_specs=VMEM,
        out_shape=jax.ShapeDtypeStruct((ROWS, D), F32),
        compiler_params=pltpu.CompilerParams(vmem_limit_bytes=8 * MB),
        name="row_pass",
    )(scalars, own, other, partner, x, w, st, gst)


def place_kernel(s_ref, own_ref, other_ref, *refs):
    out_ref, sems = refs[-2], refs[-1]
    copies = [
        pltpu.make_async_copy(own_ref, out_ref.at[s_ref[0], :, s_ref[1]], sems.at[0]),
        pltpu.make_async_copy(other_ref, out_ref.at[s_ref[0], :, 1 - s_ref[1]], sems.at[1]),
    ]
    for copy in copies:
        copy.start()
    for copy in copies:
        copy.wait()


def place(scalars, own, other, whole):
    rest = () if whole is None else (whole,)
    return pl.pallas_call(
        place_kernel,
        in_specs=[SMEM, VMEM, VMEM] + [pl.BlockSpec(memory_space=pltpu.HBM)] * len(rest),
        out_specs=pl.BlockSpec(memory_space=pltpu.HBM),
        out_shape=jax.ShapeDtypeStruct((2, 8, 2, ROWS, D), BF16),
        scratch_shapes=[pltpu.SemaphoreType.DMA((2,))],
        input_output_aliases={3: 0} if rest else {},
        compiler_params=pltpu.CompilerParams(vmem_limit_bytes=4 * MB),
        name="place",
    )(scalars, own, other, *rest)


CORE_PERM = [(i, i ^ 1) for i in range(DP)]
Y_PERM = [(i, i ^ 16) for i in range(DP)]
Z_GROUPS = [[y * 16 + z * 2 + c for z in range(8)] for y in range(2) for c in range(2)]


def exchange(x, axis, groups=None):
    return lax.all_to_all(x, axis, 0, 0, axis_index_groups=groups, tiled=True)


def doubled(x, bit):
    other = lax.ppermute(x, "dp", [(i, i ^ bit) for i in range(DP)])
    return lax.optimization_barrier(jnp.concatenate([x, other], axis=0))


def swap(x, bit):
    return lax.ppermute(x, "proto", [(i, i ^ bit) for i in range(PR)])


def inner(feature_matrix, tangent_embed, anchor_matrix, anchor_perturbation, codes, partner_lookup):
    dp = lax.axis_index("dp")
    q = lax.axis_index("proto")
    core = dp % 2
    y = dp // 16
    partner = partner_lookup.reshape(ROWS, 1)
    qs = q.reshape(1)

    block = mass_pass(qs, codes, tangent_embed)
    table = exchange(block, "dp")
    e, u, cst, st, h_part = score_pass(feature_matrix, tangent_embed, anchor_matrix, anchor_perturbation, codes)

    received = exchange(pick(qs, table, partner, st, h_part), "proto")
    x, w = embed_pass(e, u, anchor_matrix, anchor_perturbation, cst, st)
    received, x, w = lax.optimization_barrier((received, x, w))
    f12, swt, gst, h_own = stats_pass(received, feature_matrix, tangent_embed, st, cst)

    mine_far, send_far = proto_pass(jnp.stack([core, 1 - y]), f12, swt, u, e, codes)
    got_far = lax.ppermute(send_far, "dp", CORE_PERM)
    to_y = (mine_far + got_far.astype(F32)).astype(BF16)
    from_far = lax.ppermute(to_y, "dp", Y_PERM)
    f12, swt, to_y, h_own = lax.optimization_barrier((f12, swt, to_y, h_own))
    table = doubled(h_own, 8)
    mine_near, send_near = proto_pass(jnp.stack([core, y]), f12, swt, u, e, codes)
    table = doubled(table, 4)
    got_near = lax.ppermute(send_near, "dp", CORE_PERM)
    table = doubled(table, 2)
    quarter = (mine_near + got_near.astype(F32) + from_far.astype(F32)).astype(BF16)
    pieces = exchange(quarter, "dp", Z_GROUPS)
    table = doubled(table, 16)
    other = lax.ppermute(table, "dp", CORE_PERM)
    embed = row_pass(jnp.stack([q, dp]), table, other, partner, x, w, st, gst)
    final = final_pass(pieces)

    swapped = swap(embed, 4)
    along_z = exchange(final, "dp", Z_GROUPS)
    from_y = lax.ppermute(along_z, "dp", Y_PERM)
    embed = embed + swapped
    swapped = swap(embed, 2)
    embed = embed + swapped
    swapped = swap(embed, 1)
    hvp_embed = (embed + swapped).astype(BF16)
    own_core = lax.ppermute(along_z, "dp", CORE_PERM)
    whole = place(jnp.stack([y, core]), along_z, own_core, None)
    far_core = lax.ppermute(from_y, "dp", CORE_PERM)
    whole = place(jnp.stack([1 - y, core]), from_y, far_core, whole)
    return (hvp_embed, whole.reshape(LOCAL, D))


def solution(mesh):
    in_specs = (
        P("dp", None),
        P("dp", None),
        P("proto", None),
        P("proto", None),
        P("dp", "proto"),
        P("dp"),
    )
    out_specs = (P("dp", None), P("proto", None))
    return jax.shard_map(inner, mesh=mesh, in_specs=in_specs, out_specs=out_specs, check_vma=False)
```

```python
import functools

import jax
import jax.numpy as jnp
from jax import lax
from jax.experimental import pallas as pl
from jax.experimental.pallas import tpu as pltpu
from jax.sharding import PartitionSpec as P


F32 = jnp.float32
BF16 = jnp.bfloat16
NT = (((1,), (1,)), ((), ()))
TN = (((0,), (0,)), ((), ()))
D = 128
ROWS = 256
LOCAL = 8192
DP = 32
PR = 8
SUB = ROWS // PR
CN = 2048
NCH = LOCAL // CN
SCALE = 0.1
RG = 16
INV = 10.0
LOG2E = 1.4426950408889634
VMEM = pl.BlockSpec(memory_space=pltpu.VMEM)
SMEM = pl.BlockSpec(memory_space=pltpu.SMEM)
HBM = pl.BlockSpec(memory_space=pltpu.HBM)
MB = 1024 * 1024


def split3(x):
    hi = x.astype(BF16).astype(F32)
    mid = (x - hi).astype(BF16).astype(F32)
    lo = (x - hi - mid).astype(BF16).astype(F32)
    return hi, mid, lo


WIDE = 4096


def mass_kernel(q_ref, codes_ref, tan_ref, blk_ref, acc):
    step = pl.program_id(0)

    @pl.when(step == 0)
    def _():
        acc[...] = jnp.zeros_like(acc)

    for g in range(ROWS // RG):
        rows = slice(g * RG, (g + 1) * RG)
        x = codes_ref[rows, :].astype(F32)
        total = x[:, :D]
        for k in range(1, WIDE // D):
            total = total + x[:, k * D : (k + 1) * D]
        acc[rows, :] += total

    @pl.when(step == LOCAL // WIDE - 1)
    def _():
        mass = jnp.sum(jnp.transpose(acc[...]), axis=0, keepdims=True)
        hi, mid, lo = split3(mass)
        parts = jnp.concatenate([hi, mid, lo, jnp.zeros((5, ROWS), F32)], axis=0)
        parts = jnp.concatenate([parts[:, :D], parts[:, D:]], axis=0).astype(BF16)
        rows = tan_ref[pl.ds(pl.multiple_of(q_ref[0] * SUB, SUB), SUB), :]
        block = jnp.concatenate([rows, parts], axis=0)
        for i in range(DP):
            blk_ref[i] = block


def mass_pass(q, codes, tan):
    return pl.pallas_call(
        mass_kernel,
        grid=(LOCAL // WIDE,),
        in_specs=[
            SMEM,
            pl.BlockSpec((ROWS, WIDE), lambda c: (0, c)),
            pl.BlockSpec((ROWS, D), lambda c: (0, 0)),
        ],
        out_specs=pl.BlockSpec((DP, SUB + 16, D), lambda c: (0, 0, 0)),
        out_shape=jax.ShapeDtypeStruct((DP, SUB + 16, D), BF16),
        scratch_shapes=[pltpu.VMEM((ROWS, D), F32)],
        cost_estimate=pl.CostEstimate(flops=ROWS * LOCAL, bytes_accessed=5 << 20, transcendentals=0),
        compiler_params=pltpu.CompilerParams(vmem_limit_bytes=56 * MB),
        name="mass_pass",
    )(q, codes, tan)


def score_kernel(f_ref, tan_ref, a_ref, p_ref, codes_ref, e_ref, u_ref, cst_ref, st_ref, s_sc, t_sc, run, acc):
    step = pl.program_id(0)
    f = f_ref[...]
    s_sc[...] = lax.dot_general(f, a_ref[...], NT, preferred_element_type=F32)
    left = jnp.concatenate([tan_ref[...], f], axis=1)
    right = jnp.concatenate([a_ref[...], p_ref[...]], axis=1)
    t_sc[...] = lax.dot_general(left, right, NT, preferred_element_type=F32)

    @pl.when(step == 0)
    def _():
        run[0] = jnp.full((ROWS, D), -jnp.inf, F32)
        run[1] = jnp.zeros((ROWS, D), F32)
        run[2] = jnp.zeros((ROWS, D), F32)
        acc[...] = jnp.zeros_like(acc)

    acc[...] += jnp.dot(codes_ref[...], p_ref[...], preferred_element_type=F32)
    st_ref[:, D:] = acc[...]
    lane = lax.broadcasted_iota(jnp.int32, (RG, D), 1)
    for g in range(ROWS // RG):
        rows = slice(g * RG, (g + 1) * RG)
        s = s_sc[rows, :]
        t = t_sc[rows, :]
        top = jnp.max(s, axis=1, keepdims=True)
        e = jnp.exp2((s - top) * (INV * LOG2E))
        z = jnp.sum(e, axis=1, keepdims=True)
        et = jnp.sum(e * t, axis=1, keepdims=True)
        mean = et / z
        e_ref[rows, :] = e.astype(BF16)
        u_ref[rows, :] = (e * (t - mean)).astype(BF16)
        top = top * INV
        cst_ref[0, rows, :] = jnp.where(lane == 0, top, mean * INV)
        old = run[0, rows, :]
        new = jnp.maximum(old, top)
        alpha = jnp.exp(old - new)
        beta = jnp.exp(top - new)
        z_run = run[1, rows, :] * alpha + beta * z
        et_run = run[2, rows, :] * alpha + beta * (et * INV)
        run[0, rows, :] = new
        run[1, rows, :] = z_run
        run[2, rows, :] = et_run
        st_ref[rows, :D] = jnp.where(lane == 0, new, jnp.where(lane == 1, z_run, et_run))


def score_pass(f, tan, a, p, codes):
    return pl.pallas_call(
        score_kernel,
        grid=(NCH,),
        in_specs=[
            pl.BlockSpec((ROWS, D), lambda c: (0, 0)),
            pl.BlockSpec((ROWS, D), lambda c: (0, 0)),
            pl.BlockSpec((CN, D), lambda c: (c, 0)),
            pl.BlockSpec((CN, D), lambda c: (c, 0)),
            pl.BlockSpec((ROWS, CN), lambda c: (0, c)),
        ],
        out_specs=[
            pl.BlockSpec((ROWS, CN), lambda c: (0, c)),
            pl.BlockSpec((ROWS, CN), lambda c: (0, c)),
            pl.BlockSpec((1, ROWS, D), lambda c: (c, 0, 0)),
            pl.BlockSpec((ROWS, 2 * D), lambda c: (0, 0)),
        ],
        out_shape=[
            jax.ShapeDtypeStruct((ROWS, LOCAL), BF16),
            jax.ShapeDtypeStruct((ROWS, LOCAL), BF16),
            jax.ShapeDtypeStruct((NCH, ROWS, D), F32),
            jax.ShapeDtypeStruct((ROWS, 2 * D), F32),
        ],
        scratch_shapes=[
            pltpu.VMEM((ROWS, CN), F32),
            pltpu.VMEM((ROWS, CN), F32),
            pltpu.VMEM((3, ROWS, D), F32),
            pltpu.VMEM((ROWS, D), F32),
        ],
        cost_estimate=pl.CostEstimate(flops=10 * ROWS * LOCAL * D * 2, bytes_accessed=12 << 20, transcendentals=ROWS * LOCAL),
        compiler_params=pltpu.CompilerParams(vmem_limit_bytes=56 * MB),
        name="score_pass",
    )(f, tan, a, p, codes)


def embed_kernel(e_ref, u_ref, a_ref, p_ref, cst_ref, st_ref, x_ref, w_ref):
    @pl.when(pl.program_id(0) == 0)
    def _():
        x_ref[...] = jnp.zeros_like(x_ref)
        w_ref[...] = jnp.zeros_like(w_ref)

    e = e_ref[...]
    both = jnp.dot(e, jnp.concatenate([a_ref[...], p_ref[...]], axis=1), preferred_element_type=F32)
    ua = jnp.dot(u_ref[...], a_ref[...], preferred_element_type=F32)
    ea = both[:, :D]
    beta = jnp.exp(cst_ref[0, :, 0:1] - st_ref[:, 0:1])
    mean = cst_ref[0, :, 1:2]
    x_ref[...] += beta * (INV * ua + both[:, D:] + mean * ea)
    w_ref[...] += beta * ea


def embed_pass(e, u, a, p, cst, st):
    return pl.pallas_call(
        embed_kernel,
        grid=(NCH,),
        in_specs=[
            pl.BlockSpec((ROWS, CN), lambda c: (0, c)),
            pl.BlockSpec((ROWS, CN), lambda c: (0, c)),
            pl.BlockSpec((CN, D), lambda c: (c, 0)),
            pl.BlockSpec((CN, D), lambda c: (c, 0)),
            pl.BlockSpec((1, ROWS, D), lambda c: (c, 0, 0)),
            pl.BlockSpec((ROWS, D), lambda c: (0, 0)),
        ],
        out_specs=[
            pl.BlockSpec((ROWS, D), lambda c: (0, 0)),
            pl.BlockSpec((ROWS, D), lambda c: (0, 0)),
        ],
        out_shape=[jax.ShapeDtypeStruct((ROWS, D), F32)] * 2,
        cost_estimate=pl.CostEstimate(flops=6 * ROWS * LOCAL * D * 2, bytes_accessed=12 << 20, transcendentals=0),
        compiler_params=pltpu.CompilerParams(vmem_limit_bytes=56 * MB),
        name="embed_pass",
    )(e, u, a, p, cst, st)


STAT = 16
PAY = ROWS + 2 * STAT + SUB


def pick_kernel(q_ref, tab_ref, part_ref, st_ref, pay_ref):
    q = q_ref[0]
    partner = part_ref[...]
    group = partner // ROWS
    row = partner % ROWS
    mine = (row // SUB) == q
    column = jnp.where(mine, group * SUB + row % SUB, -1)
    hot = (lax.broadcasted_iota(jnp.int32, (ROWS, DP * SUB), 1) == column).astype(F32).astype(BF16)
    table = tab_ref[:, :SUB, :].reshape(DP * SUB, D)
    rows = jnp.dot(hot, table, preferred_element_type=F32).astype(BF16)

    hot_group = (lax.broadcasted_iota(jnp.int32, (ROWS, DP), 1) == group).astype(F32).astype(BF16)
    mass_rows = tab_ref[:, SUB:, :].astype(F32)
    mass = jnp.zeros((ROWS, ROWS), F32)
    for k in (2, 1, 0):
        piece = jnp.concatenate([mass_rows[:, k, :], mass_rows[:, 8 + k, :]], axis=1).astype(BF16)
        mass = mass + jnp.dot(hot_group, piece, preferred_element_type=F32)
    here = lax.broadcasted_iota(jnp.int32, (ROWS, ROWS), 1) == row
    mass = jnp.sum(jnp.where(here, mass, 0.0), axis=1, keepdims=True)

    lane = lax.broadcasted_iota(jnp.int32, (ROWS, D), 1)
    stats = jnp.where(lane == 3, mass, st_ref[:, :D])
    flat = jnp.transpose(stats)[:4, :]
    hi, mid, lo = split3(flat)
    flat = jnp.concatenate([hi, mid, lo, jnp.zeros((STAT - 12, ROWS), F32)], axis=0)
    flat = jnp.concatenate([flat[:, :D], flat[:, D:]], axis=0).astype(BF16)
    payload = jnp.concatenate([rows, flat], axis=0)
    for i in range(PR):
        pay_ref[i, : ROWS + 2 * STAT, :] = payload
        pay_ref[i, ROWS + 2 * STAT :, :] = st_ref[i * SUB : (i + 1) * SUB, D:].astype(BF16)


def pick(q, tab, partner, st):
    return pl.pallas_call(
        pick_kernel,
        in_specs=[SMEM, VMEM, VMEM, VMEM],
        out_specs=VMEM,
        out_shape=jax.ShapeDtypeStruct((PR, PAY, D), BF16),
        compiler_params=pltpu.CompilerParams(vmem_limit_bytes=10 * MB),
        name="pick",
    )(q, tab, partner, st)


def stats_kernel(rec_ref, f_ref, tan_ref, cst_ref, f12_ref, gst_ref, h_ref):
    total = jnp.zeros((ROWS, D), F32)
    h = jnp.zeros((SUB, D), F32)
    flats = []
    for i in range(PR):
        total = total + rec_ref[i, :ROWS, :].astype(F32)
        flat = rec_ref[i, ROWS : ROWS + 2 * STAT, :].astype(F32)
        flat = jnp.concatenate([flat[:STAT], flat[STAT:]], axis=1)
        flats.append((flat[0:4] + flat[4:8]) + flat[8:12])
        h = h + rec_ref[i, ROWS + 2 * STAT :, :].astype(F32)
    f12_ref[2 * NCH] = (total * SCALE).astype(BF16)
    h_ref[...] = h.astype(BF16)
    top = flats[0][0:1]
    for i in range(1, PR):
        top = jnp.maximum(top, flats[i][0:1])
    z = jnp.zeros((1, ROWS), F32)
    et = jnp.zeros((1, ROWS), F32)
    mass = jnp.zeros((1, ROWS), F32)
    for i in range(PR):
        shift = jnp.exp(flats[i][0:1] - top)
        z = z + shift * flats[i][1:2]
        et = et + shift * flats[i][2:3]
        mass = mass + flats[i][3:4]
    rows = jnp.concatenate([top, et / z, SCALE * mass / z, jnp.zeros((D - 3, ROWS), F32)], axis=0)
    cols = jnp.transpose(rows)
    gst_ref[...] = cols
    top = cols[:, 0:1]
    mean = cols[:, 1:2]
    weight = cols[:, 2:3]
    f = f_ref[...].astype(F32)
    tan = tan_ref[...].astype(F32)
    for c in range(NCH):
        scale = weight * jnp.exp(cst_ref[c, :, 0:1] - top)
        f12_ref[2 * c] = (INV * scale * f).astype(BF16)
        f12_ref[2 * c + 1] = (scale * ((cst_ref[c, :, 1:2] - mean) * f + tan)).astype(BF16)


def stats_pass(rec, f, tan, cst):
    return pl.pallas_call(
        stats_kernel,
        in_specs=[VMEM] * 4,
        out_specs=[VMEM] * 3,
        out_shape=[
            jax.ShapeDtypeStruct((2 * NCH + 1, ROWS, D), BF16),
            jax.ShapeDtypeStruct((ROWS, D), F32),
            jax.ShapeDtypeStruct((SUB, D), BF16),
        ],
        compiler_params=pltpu.CompilerParams(vmem_limit_bytes=10 * MB),
        name="stats_pass",
    )(rec, f, tan, cst)


def proto_kernel(s_ref, f12_ref, swt_ref, u_ref, e_ref, codes_ref, mine_ref, send_ref):
    res = lax.dot_general(u_ref[...], f12_ref[0], TN, preferred_element_type=F32)
    res = res + lax.dot_general(e_ref[...], f12_ref[1], TN, preferred_element_type=F32)
    res = res - lax.dot_general(codes_ref[...], swt_ref[0], TN, preferred_element_type=F32)
    first = s_ref[0] == 0
    for b in range(CN // (2 * ROWS)):
        even = res[2 * b * ROWS : (2 * b + 1) * ROWS]
        odd = res[(2 * b + 1) * ROWS : (2 * b + 2) * ROWS]
        mine_ref[b] = jnp.where(first, even, odd)
        send_ref[b] = jnp.where(first, odd, even).astype(BF16)


def proto_pass(scalars, f12, u, e, codes):
    nb = CN // (2 * ROWS)
    steps = NCH // 2
    wide = pl.BlockSpec((ROWS, CN), lambda c, s: (0, s[1] * steps + c))
    return pl.pallas_call(
        proto_kernel,
        grid_spec=pltpu.PrefetchScalarGridSpec(
            num_scalar_prefetch=1,
            grid=(steps,),
            in_specs=[
                pl.BlockSpec((2, ROWS, D), lambda c, s: (s[1] * steps + c, 0, 0)),
                pl.BlockSpec((1, ROWS, D), lambda c, s: (2 * NCH, 0, 0)),
                wide,
                wide,
                wide,
            ],
            out_specs=[
                pl.BlockSpec((nb, ROWS, D), lambda c, s: (c, 0, 0)),
                pl.BlockSpec((nb, ROWS, D), lambda c, s: (c, 0, 0)),
            ],
        ),
        out_shape=[
            jax.ShapeDtypeStruct((8, ROWS, D), F32),
            jax.ShapeDtypeStruct((8, ROWS, D), BF16),
        ],
        cost_estimate=pl.CostEstimate(flops=3 * ROWS * LOCAL * D * 2, bytes_accessed=9 << 20, transcendentals=0),
        compiler_params=pltpu.CompilerParams(vmem_limit_bytes=56 * MB),
        name="proto_pass",
    )(scalars, f12, f12, u, e, codes)


def final_kernel(pieces_ref, out_ref):
    total = pieces_ref[0].astype(F32)
    for i in range(1, 8):
        total = total + pieces_ref[i].astype(F32)
    total = total.astype(BF16)
    for i in range(8):
        out_ref[i] = total


def final_pass(pieces):
    return pl.pallas_call(
        final_kernel,
        in_specs=[VMEM],
        out_specs=VMEM,
        out_shape=jax.ShapeDtypeStruct((8, ROWS, D), BF16),
        compiler_params=pltpu.CompilerParams(vmem_limit_bytes=8 * MB),
        name="final_pass",
    )(pieces)


def row_kernel(s_ref, own_ref, other_ref, part_ref, x_ref, w_ref, st_ref, gst_ref, emb_ref):
    q = s_ref[0]
    partner = part_ref[...]
    away = (partner // ROWS) ^ s_ref[1]
    block = (away & 1) + 2 * ((away >> 3) & 1) + 4 * ((away >> 2) & 1) + 8 * ((away >> 1) & 1) + 16 * ((away >> 4) & 1)
    row = partner % ROWS
    column = jnp.where((row // SUB) == q, block * SUB + row % SUB, -1)
    hot = (lax.broadcasted_iota(jnp.int32, (ROWS, DP * SUB), 1) == column).astype(F32).astype(BF16)
    table = jnp.concatenate([own_ref[...], other_ref[...]], axis=0)
    h = jnp.dot(hot, table, preferred_element_type=F32)
    scale = gst_ref[:, 2:3] * jnp.exp(st_ref[:, 0:1] - gst_ref[:, 0:1])
    emb_ref[...] = scale * (x_ref[...] - gst_ref[:, 1:2] * w_ref[...]) - SCALE * h


def row_pass(scalars, own, other, partner, x, w, st, gst):
    return pl.pallas_call(
        row_kernel,
        in_specs=[SMEM] + [VMEM] * 7,
        out_specs=VMEM,
        out_shape=jax.ShapeDtypeStruct((ROWS, D), F32),
        compiler_params=pltpu.CompilerParams(vmem_limit_bytes=8 * MB),
        name="row_pass",
    )(scalars, own, other, partner, x, w, st, gst)


def place_kernel(count, s_ref, *refs):
    out_ref, sems = refs[-2], refs[-1]
    copies = []
    for i in range(count):
        for part in range(4):
            copies.append(pltpu.make_async_copy(
                refs[i].at[2 * part : 2 * part + 2],
                out_ref.at[s_ref[0], 2 * part : 2 * part + 2, s_ref[1 + i]],
                sems.at[4 * i + part],
            ))
    for copy in copies:
        copy.start()
    for copy in copies:
        copy.wait()


def place(scalars, blocks, whole):
    rest = () if whole is None else (whole,)
    return pl.pallas_call(
        functools.partial(place_kernel, len(blocks)),
        in_specs=[SMEM] + [VMEM] * len(blocks) + [HBM] * len(rest),
        out_specs=HBM,
        out_shape=jax.ShapeDtypeStruct((2, 8, 2, ROWS, D), BF16),
        scratch_shapes=[pltpu.SemaphoreType.DMA((8,))],
        input_output_aliases={1 + len(blocks): 0} if rest else {},
        compiler_params=pltpu.CompilerParams(vmem_limit_bytes=4 * MB),
        name="place",
    )(scalars, *blocks, *rest)


CORE_PERM = [(i, i ^ 1) for i in range(DP)]
Y_PERM = [(i, i ^ 16) for i in range(DP)]
Z_GROUPS = [[y * 16 + z * 2 + c for z in range(8)] for y in range(2) for c in range(2)]


def exchange(x, axis, groups=None):
    return lax.all_to_all(x, axis, 0, 0, axis_index_groups=groups, tiled=True)


def doubled(x, bit):
    other = lax.ppermute(x, "dp", [(i, i ^ bit) for i in range(DP)])
    return lax.optimization_barrier(jnp.concatenate([x, other], axis=0))


def swap(x, bit):
    return lax.ppermute(x, "proto", [(i, i ^ bit) for i in range(PR)])


def inner(feature_matrix, tangent_embed, anchor_matrix, anchor_perturbation, codes, partner_lookup):
    dp = lax.axis_index("dp")
    q = lax.axis_index("proto")
    core = dp % 2
    y = dp // 16
    partner = partner_lookup.reshape(ROWS, 1)
    qs = q.reshape(1)

    block = mass_pass(qs, codes, tangent_embed)
    table = exchange(block, "dp")
    e, u, cst, st = score_pass(feature_matrix, tangent_embed, anchor_matrix, anchor_perturbation, codes)

    received = exchange(pick(qs, table, partner, st), "proto")
    x, w = embed_pass(e, u, anchor_matrix, anchor_perturbation, cst, st)
    received, x, w = lax.optimization_barrier((received, x, w))
    f12, gst, h_own = stats_pass(received, feature_matrix, tangent_embed, cst)

    table = doubled(h_own, 1)
    mine_far, send_far = proto_pass(jnp.stack([core, 1 - y]), f12, u, e, codes)
    table = doubled(table, 8)
    got_far = lax.ppermute(send_far, "dp", CORE_PERM)
    to_y = (mine_far + got_far.astype(F32)).astype(BF16)
    from_far = lax.ppermute(to_y, "dp", Y_PERM)
    f12, to_y = lax.optimization_barrier((f12, to_y))
    table = doubled(table, 4)
    mine_near, send_near = proto_pass(jnp.stack([core, y]), f12, u, e, codes)
    got_near = lax.ppermute(send_near, "dp", CORE_PERM)
    table = doubled(table, 2)
    quarter = (mine_near + got_near.astype(F32) + from_far.astype(F32)).astype(BF16)
    pieces = exchange(quarter, "dp", Z_GROUPS)
    other = lax.ppermute(table, "dp", Y_PERM)
    embed = row_pass(jnp.stack([q, dp]), table, other, partner, x, w, st, gst)
    final = final_pass(pieces)

    swapped = swap(embed, 1)
    along_z = exchange(final, "dp", Z_GROUPS)
    from_y = lax.ppermute(along_z, "dp", Y_PERM)
    embed = embed + swapped
    swapped = swap(embed, 4)
    embed = embed + swapped
    swapped = swap(embed, 2)
    hvp_embed = (embed + swapped).astype(BF16)
    own_core = lax.ppermute(along_z, "dp", CORE_PERM)
    whole = place(jnp.stack([y, core, 1 - core]), (along_z, own_core), None)
    far_core = lax.ppermute(from_y, "dp", CORE_PERM)
    whole = place(jnp.stack([1 - y, core]), (from_y,), whole)
    whole = place(jnp.stack([1 - y, 1 - core]), (far_core,), whole)
    return (hvp_embed, whole.reshape(LOCAL, D))


def solution(mesh):
    in_specs = (
        P("dp", None),
        P("dp", None),
        P("proto", None),
        P("proto", None),
        P("dp", "proto"),
        P("dp"),
    )
    out_specs = (P("dp", None), P("proto", None))
    return jax.shard_map(inner, mesh=mesh, in_specs=in_specs, out_specs=out_specs, check_vma=False)
```

```python
import functools

import jax
import jax.numpy as jnp
from jax import lax
from jax.experimental import pallas as pl
from jax.experimental.pallas import tpu as pltpu
from jax.sharding import PartitionSpec as P


F32 = jnp.float32
BF16 = jnp.bfloat16
NT = (((1,), (1,)), ((), ()))
TN = (((0,), (0,)), ((), ()))
D = 128
ROWS = 256
LOCAL = 8192
DP = 32
PR = 8
SUB = ROWS // PR
CN = 2048
NCH = LOCAL // CN
SCALE = 0.1
RG = 16
INV = 10.0
LOG2E = 1.4426950408889634
VMEM = pl.BlockSpec(memory_space=pltpu.VMEM)
SMEM = pl.BlockSpec(memory_space=pltpu.SMEM)
HBM = pl.BlockSpec(memory_space=pltpu.HBM)
MB = 1024 * 1024


def split3(x):
    hi = x.astype(BF16).astype(F32)
    mid = (x - hi).astype(BF16).astype(F32)
    lo = (x - hi - mid).astype(BF16).astype(F32)
    return hi, mid, lo


WIDE = 4096


def mass_kernel(q_ref, codes_ref, tan_ref, blk_ref, acc):
    step = pl.program_id(0)

    @pl.when(step == 0)
    def _():
        acc[...] = jnp.zeros_like(acc)

    for g in range(ROWS // RG):
        rows = slice(g * RG, (g + 1) * RG)
        x = codes_ref[rows, :].astype(F32)
        total = x[:, :D]
        for k in range(1, WIDE // D):
            total = total + x[:, k * D : (k + 1) * D]
        acc[rows, :] += total

    @pl.when(step == LOCAL // WIDE - 1)
    def _():
        mass = jnp.sum(jnp.transpose(acc[...]), axis=0, keepdims=True)
        hi, mid, lo = split3(mass)
        parts = jnp.concatenate([hi, mid, lo, jnp.zeros((5, ROWS), F32)], axis=0)
        parts = jnp.concatenate([parts[:, :D], parts[:, D:]], axis=0).astype(BF16)
        rows = tan_ref[pl.ds(pl.multiple_of(q_ref[0] * SUB, SUB), SUB), :]
        block = jnp.concatenate([rows, parts], axis=0)
        for i in range(DP):
            blk_ref[i] = block


def mass_pass(q, codes, tan):
    return pl.pallas_call(
        mass_kernel,
        grid=(LOCAL // WIDE,),
        in_specs=[
            SMEM,
            pl.BlockSpec((ROWS, WIDE), lambda c: (0, c)),
            pl.BlockSpec((ROWS, D), lambda c: (0, 0)),
        ],
        out_specs=pl.BlockSpec((DP, SUB + 16, D), lambda c: (0, 0, 0)),
        out_shape=jax.ShapeDtypeStruct((DP, SUB + 16, D), BF16),
        scratch_shapes=[pltpu.VMEM((ROWS, D), F32)],
        cost_estimate=pl.CostEstimate(flops=ROWS * LOCAL, bytes_accessed=5 << 20, transcendentals=0),
        compiler_params=pltpu.CompilerParams(vmem_limit_bytes=56 * MB),
        name="mass_pass",
    )(q, codes, tan)


def score_kernel(f_ref, tan_ref, a_ref, p_ref, codes_ref, e_ref, u_ref, cst_ref, st_ref, s_sc, t_sc, run, acc):
    step = pl.program_id(0)
    f = f_ref[...]
    s_sc[...] = lax.dot_general(f, a_ref[...], NT, preferred_element_type=F32)
    left = jnp.concatenate([tan_ref[...], f], axis=1)
    right = jnp.concatenate([a_ref[...], p_ref[...]], axis=1)
    t_sc[...] = lax.dot_general(left, right, NT, preferred_element_type=F32)

    @pl.when(step == 0)
    def _():
        run[0] = jnp.full((ROWS, D), -jnp.inf, F32)
        run[1] = jnp.zeros((ROWS, D), F32)
        run[2] = jnp.zeros((ROWS, D), F32)
        acc[...] = jnp.zeros_like(acc)

    acc[...] += jnp.dot(codes_ref[...], p_ref[...], preferred_element_type=F32)
    st_ref[:, D:] = acc[...]
    lane = lax.broadcasted_iota(jnp.int32, (RG, D), 1)
    for g in range(ROWS // RG):
        rows = slice(g * RG, (g + 1) * RG)
        s = s_sc[rows, :]
        t = t_sc[rows, :]
        top = jnp.max(s, axis=1, keepdims=True)
        e = jnp.exp2((s - top) * (INV * LOG2E))
        z = jnp.sum(e, axis=1, keepdims=True)
        et = jnp.sum(e * t, axis=1, keepdims=True)
        mean = et / z
        e_ref[rows, :] = e.astype(BF16)
        u_ref[rows, :] = (e * (t - mean)).astype(BF16)
        top = top * INV
        cst_ref[0, rows, :] = jnp.where(lane == 0, top, mean * INV)
        old = run[0, rows, :]
        new = jnp.maximum(old, top)
        alpha = jnp.exp(old - new)
        beta = jnp.exp(top - new)
        z_run = run[1, rows, :] * alpha + beta * z
        et_run = run[2, rows, :] * alpha + beta * (et * INV)
        run[0, rows, :] = new
        run[1, rows, :] = z_run
        run[2, rows, :] = et_run
        st_ref[rows, :D] = jnp.where(lane == 0, new, jnp.where(lane == 1, z_run, et_run))


def score_pass(f, tan, a, p, codes):
    return pl.pallas_call(
        score_kernel,
        grid=(NCH,),
        in_specs=[
            pl.BlockSpec((ROWS, D), lambda c: (0, 0)),
            pl.BlockSpec((ROWS, D), lambda c: (0, 0)),
            pl.BlockSpec((CN, D), lambda c: (c, 0)),
            pl.BlockSpec((CN, D), lambda c: (c, 0)),
            pl.BlockSpec((ROWS, CN), lambda c: (0, c)),
        ],
        out_specs=[
            pl.BlockSpec((ROWS, CN), lambda c: (0, c)),
            pl.BlockSpec((ROWS, CN), lambda c: (0, c)),
            pl.BlockSpec((1, ROWS, D), lambda c: (c, 0, 0)),
            pl.BlockSpec((ROWS, 2 * D), lambda c: (0, 0)),
        ],
        out_shape=[
            jax.ShapeDtypeStruct((ROWS, LOCAL), BF16),
            jax.ShapeDtypeStruct((ROWS, LOCAL), BF16),
            jax.ShapeDtypeStruct((NCH, ROWS, D), F32),
            jax.ShapeDtypeStruct((ROWS, 2 * D), F32),
        ],
        scratch_shapes=[
            pltpu.VMEM((ROWS, CN), F32),
            pltpu.VMEM((ROWS, CN), F32),
            pltpu.VMEM((3, ROWS, D), F32),
            pltpu.VMEM((ROWS, D), F32),
        ],
        cost_estimate=pl.CostEstimate(flops=10 * ROWS * LOCAL * D * 2, bytes_accessed=12 << 20, transcendentals=ROWS * LOCAL),
        compiler_params=pltpu.CompilerParams(vmem_limit_bytes=56 * MB),
        name="score_pass",
    )(f, tan, a, p, codes)


def embed_kernel(e_ref, u_ref, a_ref, p_ref, cst_ref, st_ref, x_ref, w_ref):
    @pl.when(pl.program_id(0) == 0)
    def _():
        x_ref[...] = jnp.zeros_like(x_ref)
        w_ref[...] = jnp.zeros_like(w_ref)

    e = e_ref[...]
    both = jnp.dot(e, jnp.concatenate([a_ref[...], p_ref[...]], axis=1), preferred_element_type=F32)
    ua = jnp.dot(u_ref[...], a_ref[...], preferred_element_type=F32)
    ea = both[:, :D]
    beta = jnp.exp(cst_ref[0, :, 0:1] - st_ref[:, 0:1])
    mean = cst_ref[0, :, 1:2]
    x_ref[...] += beta * (INV * ua + both[:, D:] + mean * ea)
    w_ref[...] += beta * ea


def embed_pass(e, u, a, p, cst, st):
    return pl.pallas_call(
        embed_kernel,
        grid=(NCH,),
        in_specs=[
            pl.BlockSpec((ROWS, CN), lambda c: (0, c)),
            pl.BlockSpec((ROWS, CN), lambda c: (0, c)),
            pl.BlockSpec((CN, D), lambda c: (c, 0)),
            pl.BlockSpec((CN, D), lambda c: (c, 0)),
            pl.BlockSpec((1, ROWS, D), lambda c: (c, 0, 0)),
            pl.BlockSpec((ROWS, D), lambda c: (0, 0)),
        ],
        out_specs=[
            pl.BlockSpec((ROWS, D), lambda c: (0, 0)),
            pl.BlockSpec((ROWS, D), lambda c: (0, 0)),
        ],
        out_shape=[jax.ShapeDtypeStruct((ROWS, D), F32)] * 2,
        cost_estimate=pl.CostEstimate(flops=6 * ROWS * LOCAL * D * 2, bytes_accessed=12 << 20, transcendentals=0),
        compiler_params=pltpu.CompilerParams(vmem_limit_bytes=56 * MB),
        name="embed_pass",
    )(e, u, a, p, cst, st)


STAT = 16
PAY = ROWS + 2 * STAT + SUB


def pick_kernel(q_ref, tab_ref, part_ref, st_ref, pay_ref):
    q = q_ref[0]
    partner = part_ref[...]
    group = partner // ROWS
    row = partner % ROWS
    mine = (row // SUB) == q
    column = jnp.where(mine, group * SUB + row % SUB, -1)
    hot = (lax.broadcasted_iota(jnp.int32, (ROWS, DP * SUB), 1) == column).astype(F32).astype(BF16)
    table = tab_ref[:, :SUB, :].reshape(DP * SUB, D)
    rows = jnp.dot(hot, table, preferred_element_type=F32).astype(BF16)

    hot_group = (lax.broadcasted_iota(jnp.int32, (ROWS, DP), 1) == group).astype(F32).astype(BF16)
    mass_rows = tab_ref[:, SUB:, :].astype(F32)
    mass = jnp.zeros((ROWS, ROWS), F32)
    for k in (2, 1, 0):
        piece = jnp.concatenate([mass_rows[:, k, :], mass_rows[:, 8 + k, :]], axis=1).astype(BF16)
        mass = mass + jnp.dot(hot_group, piece, preferred_element_type=F32)
    here = lax.broadcasted_iota(jnp.int32, (ROWS, ROWS), 1) == row
    mass = jnp.sum(jnp.where(here, mass, 0.0), axis=1, keepdims=True)

    lane = lax.broadcasted_iota(jnp.int32, (ROWS, D), 1)
    stats = jnp.where(lane == 3, mass, st_ref[:, :D])
    flat = jnp.transpose(stats)[:4, :]
    hi, mid, lo = split3(flat)
    flat = jnp.concatenate([hi, mid, lo, jnp.zeros((STAT - 12, ROWS), F32)], axis=0)
    flat = jnp.concatenate([flat[:, :D], flat[:, D:]], axis=0).astype(BF16)
    payload = jnp.concatenate([rows, flat], axis=0)
    for i in range(PR):
        pay_ref[i, : ROWS + 2 * STAT, :] = payload
        pay_ref[i, ROWS + 2 * STAT :, :] = st_ref[i * SUB : (i + 1) * SUB, D:].astype(BF16)


def pick(q, tab, partner, st):
    return pl.pallas_call(
        pick_kernel,
        in_specs=[SMEM, VMEM, VMEM, VMEM],
        out_specs=VMEM,
        out_shape=jax.ShapeDtypeStruct((PR, PAY, D), BF16),
        compiler_params=pltpu.CompilerParams(vmem_limit_bytes=10 * MB),
        name="pick",
    )(q, tab, partner, st)


def stats_kernel(rec_ref, f_ref, tan_ref, cst_ref, f12_ref, gst_ref, h_ref):
    total = jnp.zeros((ROWS, D), F32)
    h = jnp.zeros((SUB, D), F32)
    flats = []
    for i in range(PR):
        total = total + rec_ref[i, :ROWS, :].astype(F32)
        flat = rec_ref[i, ROWS : ROWS + 2 * STAT, :].astype(F32)
        flat = jnp.concatenate([flat[:STAT], flat[STAT:]], axis=1)
        flats.append((flat[0:4] + flat[4:8]) + flat[8:12])
        h = h + rec_ref[i, ROWS + 2 * STAT :, :].astype(F32)
    f12_ref[2 * NCH] = (total * SCALE).astype(BF16)
    h_ref[...] = h.astype(BF16)
    top = flats[0][0:1]
    for i in range(1, PR):
        top = jnp.maximum(top, flats[i][0:1])
    z = jnp.zeros((1, ROWS), F32)
    et = jnp.zeros((1, ROWS), F32)
    mass = jnp.zeros((1, ROWS), F32)
    for i in range(PR):
        shift = jnp.exp(flats[i][0:1] - top)
        z = z + shift * flats[i][1:2]
        et = et + shift * flats[i][2:3]
        mass = mass + flats[i][3:4]
    rows = jnp.concatenate([top, et / z, SCALE * mass / z, jnp.zeros((D - 3, ROWS), F32)], axis=0)
    cols = jnp.transpose(rows)
    gst_ref[...] = cols
    top = cols[:, 0:1]
    mean = cols[:, 1:2]
    weight = cols[:, 2:3]
    f = f_ref[...].astype(F32)
    tan = tan_ref[...].astype(F32)
    for c in range(NCH):
        scale = weight * jnp.exp(cst_ref[c, :, 0:1] - top)
        f12_ref[2 * c] = (INV * scale * f).astype(BF16)
        f12_ref[2 * c + 1] = (scale * ((cst_ref[c, :, 1:2] - mean) * f + tan)).astype(BF16)


def stats_pass(rec, f, tan, cst):
    return pl.pallas_call(
        stats_kernel,
        in_specs=[VMEM] * 4,
        out_specs=[VMEM] * 3,
        out_shape=[
            jax.ShapeDtypeStruct((2 * NCH + 1, ROWS, D), BF16),
            jax.ShapeDtypeStruct((ROWS, D), F32),
            jax.ShapeDtypeStruct((SUB, D), BF16),
        ],
        compiler_params=pltpu.CompilerParams(vmem_limit_bytes=10 * MB),
        name="stats_pass",
    )(rec, f, tan, cst)


def proto_kernel(s_ref, f12_ref, swt_ref, u_ref, e_ref, codes_ref, mine_ref, send_ref):
    res = lax.dot_general(u_ref[...], f12_ref[0], TN, preferred_element_type=F32)
    res = res + lax.dot_general(e_ref[...], f12_ref[1], TN, preferred_element_type=F32)
    res = res - lax.dot_general(codes_ref[...], swt_ref[0], TN, preferred_element_type=F32)
    first = s_ref[0] == 0
    for b in range(CN // (2 * ROWS)):
        even = res[2 * b * ROWS : (2 * b + 1) * ROWS]
        odd = res[(2 * b + 1) * ROWS : (2 * b + 2) * ROWS]
        mine_ref[b] = jnp.where(first, even, odd)
        send_ref[b] = jnp.where(first, odd, even).astype(BF16)


def proto_pass(scalars, f12, u, e, codes):
    nb = CN // (2 * ROWS)
    steps = NCH // 2
    wide = pl.BlockSpec((ROWS, CN), lambda c, s: (0, s[1] * steps + c))
    return pl.pallas_call(
        proto_kernel,
        grid_spec=pltpu.PrefetchScalarGridSpec(
            num_scalar_prefetch=1,
            grid=(steps,),
            in_specs=[
                pl.BlockSpec((2, ROWS, D), lambda c, s: (s[1] * steps + c, 0, 0)),
                pl.BlockSpec((1, ROWS, D), lambda c, s: (2 * NCH, 0, 0)),
                wide,
                wide,
                wide,
            ],
            out_specs=[
                pl.BlockSpec((nb, ROWS, D), lambda c, s: (c, 0, 0)),
                pl.BlockSpec((nb, ROWS, D), lambda c, s: (c, 0, 0)),
            ],
        ),
        out_shape=[
            jax.ShapeDtypeStruct((8, ROWS, D), F32),
            jax.ShapeDtypeStruct((8, ROWS, D), BF16),
        ],
        cost_estimate=pl.CostEstimate(flops=3 * ROWS * LOCAL * D * 2, bytes_accessed=9 << 20, transcendentals=0),
        compiler_params=pltpu.CompilerParams(vmem_limit_bytes=56 * MB),
        name="proto_pass",
    )(scalars, f12, f12, u, e, codes)


def final_kernel(pieces_ref, out_ref):
    total = pieces_ref[0].astype(F32)
    for i in range(1, 8):
        total = total + pieces_ref[i].astype(F32)
    out_ref[...] = total.astype(BF16)


def final_pass(pieces):
    return pl.pallas_call(
        final_kernel,
        in_specs=[VMEM],
        out_specs=VMEM,
        out_shape=jax.ShapeDtypeStruct((ROWS, D), BF16),
        compiler_params=pltpu.CompilerParams(vmem_limit_bytes=8 * MB),
        name="final_pass",
    )(pieces)


def row_kernel(s_ref, own_ref, other_ref, part_ref, x_ref, w_ref, st_ref, gst_ref, emb_ref):
    q = s_ref[0]
    partner = part_ref[...]
    away = (partner // ROWS) ^ s_ref[1]
    block = (away & 1) + 2 * ((away >> 3) & 1) + 4 * ((away >> 2) & 1) + 8 * ((away >> 1) & 1) + 16 * ((away >> 4) & 1)
    row = partner % ROWS
    column = jnp.where((row // SUB) == q, block * SUB + row % SUB, -1)
    hot = (lax.broadcasted_iota(jnp.int32, (ROWS, DP * SUB), 1) == column).astype(F32).astype(BF16)
    table = jnp.concatenate([own_ref[...], other_ref[...]], axis=0)
    h = jnp.dot(hot, table, preferred_element_type=F32)
    scale = gst_ref[:, 2:3] * jnp.exp(st_ref[:, 0:1] - gst_ref[:, 0:1])
    emb_ref[...] = scale * (x_ref[...] - gst_ref[:, 1:2] * w_ref[...]) - SCALE * h


def row_pass(scalars, own, other, partner, x, w, st, gst):
    return pl.pallas_call(
        row_kernel,
        in_specs=[SMEM] + [VMEM] * 7,
        out_specs=VMEM,
        out_shape=jax.ShapeDtypeStruct((ROWS, D), F32),
        compiler_params=pltpu.CompilerParams(vmem_limit_bytes=8 * MB),
        name="row_pass",
    )(scalars, own, other, partner, x, w, st, gst)


def place_kernel(pieces, s_ref, *refs):
    out_ref, sems = refs[-2], refs[-1]
    copies = []
    for ref, (far, other, shifts) in zip(refs, pieces):
        for i, shift in enumerate(shifts):
            copies.append(pltpu.make_async_copy(
                ref.at[i],
                out_ref.at[s_ref[0] ^ far, (s_ref[1] + (8 - shift)) & 7, s_ref[2] ^ other],
                sems.at[len(copies)],
            ))
    for copy in copies:
        copy.start()
    for copy in copies:
        copy.wait()


def place(scalars, pieces, blocks, whole):
    rest = () if whole is None else (whole,)
    count = sum(len(piece[2]) for piece in pieces)
    return pl.pallas_call(
        functools.partial(place_kernel, pieces),
        in_specs=[SMEM] + [VMEM] * len(blocks) + [HBM] * len(rest),
        out_specs=HBM,
        out_shape=jax.ShapeDtypeStruct((2, 8, 2, ROWS, D), BF16),
        scratch_shapes=[pltpu.SemaphoreType.DMA((count,))],
        input_output_aliases={1 + len(blocks): 0} if rest else {},
        compiler_params=pltpu.CompilerParams(vmem_limit_bytes=4 * MB),
        name="place",
    )(scalars, *blocks, *rest)


CORE_PERM = [(i, i ^ 1) for i in range(DP)]
Y_PERM = [(i, i ^ 16) for i in range(DP)]
Z_PERMS = {k: [(i, (i & 17) | (((i >> 1) + k) % 8) << 1) for i in range(DP)] for k in range(1, 8)}
SHIFTS = ((0,), (4, 3, 5), (2, 6), (1, 7))
Z_GROUPS = [[y * 16 + z * 2 + c for z in range(8)] for y in range(2) for c in range(2)]


def exchange(x, axis, groups=None):
    return lax.all_to_all(x, axis, 0, 0, axis_index_groups=groups, tiled=True)


def doubled(x, bit):
    other = lax.ppermute(x, "dp", [(i, i ^ bit) for i in range(DP)])
    return lax.optimization_barrier(jnp.concatenate([x, other], axis=0))


def along(x, perm):
    return lax.ppermute(x, "dp", perm)


def swap(x, bit):
    return lax.ppermute(x, "proto", [(i, i ^ bit) for i in range(PR)])


def inner(feature_matrix, tangent_embed, anchor_matrix, anchor_perturbation, codes, partner_lookup):
    dp = lax.axis_index("dp")
    q = lax.axis_index("proto")
    core = dp % 2
    y = dp // 16
    partner = partner_lookup.reshape(ROWS, 1)
    qs = q.reshape(1)

    block = mass_pass(qs, codes, tangent_embed)
    table = exchange(block, "dp")
    e, u, cst, st = score_pass(feature_matrix, tangent_embed, anchor_matrix, anchor_perturbation, codes)

    received = exchange(pick(qs, table, partner, st), "proto")
    x, w = embed_pass(e, u, anchor_matrix, anchor_perturbation, cst, st)
    received, x, w = lax.optimization_barrier((received, x, w))
    f12, gst, h_own = stats_pass(received, feature_matrix, tangent_embed, cst)

    table = doubled(h_own, 1)
    mine_far, send_far = proto_pass(jnp.stack([core, 1 - y]), f12, u, e, codes)
    table = doubled(table, 8)
    got_far = lax.ppermute(send_far, "dp", CORE_PERM)
    to_y = (mine_far + got_far.astype(F32)).astype(BF16)
    from_far = lax.ppermute(to_y, "dp", Y_PERM)
    f12, to_y = lax.optimization_barrier((f12, to_y))
    table = doubled(table, 4)
    mine_near, send_near = proto_pass(jnp.stack([core, y]), f12, u, e, codes)
    got_near = lax.ppermute(send_near, "dp", CORE_PERM)
    table = doubled(table, 2)
    quarter = (mine_near + got_near.astype(F32) + from_far.astype(F32)).astype(BF16)
    pieces = exchange(quarter, "dp", Z_GROUPS)
    other = lax.ppermute(table, "dp", Y_PERM)
    embed = row_pass(jnp.stack([q, dp]), table, other, partner, x, w, st, gst)
    final = final_pass(pieces)

    first = swap(embed, 1)
    groups = [final[None]]
    for shifts in SHIFTS[1:]:
        group = [along(final, Z_PERMS[k]) for k in shifts]
        groups.append(lax.optimization_barrier(jnp.stack(group)))
    across = [along(group, Y_PERM) for group in groups]
    embed = embed + first
    second = swap(embed, 4)
    embed = embed + second
    third = swap(embed, 2)
    hvp_embed = (embed + third).astype(BF16)
    own_core = [along(group, CORE_PERM) for group in groups]
    far_core = [along(group, CORE_PERM) for group in across]
    pieces, blocks = [], []
    for i, shifts in enumerate(SHIFTS):
        pieces += [(0, 0, shifts), (0, 1, shifts), (1, 0, shifts), (1, 1, shifts)]
        blocks += [groups[i], own_core[i], across[i], far_core[i]]
    where = jnp.stack([y, (dp // 2) % 8, core])
    early = 14
    whole = place(where, pieces[:early], blocks[:early], None)
    whole = place(where, pieces[early:], blocks[early:], whole)
    return (hvp_embed, whole.reshape(LOCAL, D))


def solution(mesh):
    in_specs = (
        P("dp", None),
        P("dp", None),
        P("proto", None),
        P("proto", None),
        P("dp", "proto"),
        P("dp"),
    )
    out_specs = (P("dp", None), P("proto", None))
    return jax.shard_map(inner, mesh=mesh, in_specs=in_specs, out_specs=out_specs, check_vma=False)
```

```python
import functools

import jax
import jax.numpy as jnp
from jax import lax
from jax.experimental import pallas as pl
from jax.experimental.pallas import tpu as pltpu
from jax.sharding import PartitionSpec as P


F32 = jnp.float32
BF16 = jnp.bfloat16
NT = (((1,), (1,)), ((), ()))
TN = (((0,), (0,)), ((), ()))
D = 128
ROWS = 256
LOCAL = 8192
DP = 32
PR = 8
SUB = ROWS // PR
CN = 2048
NCH = LOCAL // CN
SCALE = 0.1
RG = 16
INV = 10.0
LOG2E = 1.4426950408889634
VMEM = pl.BlockSpec(memory_space=pltpu.VMEM)
SMEM = pl.BlockSpec(memory_space=pltpu.SMEM)
HBM = pl.BlockSpec(memory_space=pltpu.HBM)
MB = 1024 * 1024


def split3(x):
    hi = x.astype(BF16).astype(F32)
    mid = (x - hi).astype(BF16).astype(F32)
    lo = (x - hi - mid).astype(BF16).astype(F32)
    return hi, mid, lo


WIDE = 4096


def mass_kernel(q_ref, codes_ref, tan_ref, blk_ref, acc):
    step = pl.program_id(0)

    @pl.when(step == 0)
    def _():
        acc[...] = jnp.zeros_like(acc)

    for g in range(ROWS // RG):
        rows = slice(g * RG, (g + 1) * RG)
        x = codes_ref[rows, :].astype(F32)
        total = x[:, :D]
        for k in range(1, WIDE // D):
            total = total + x[:, k * D : (k + 1) * D]
        acc[rows, :] += total

    @pl.when(step == LOCAL // WIDE - 1)
    def _():
        mass = jnp.sum(jnp.transpose(acc[...]), axis=0, keepdims=True)
        hi, mid, lo = split3(mass)
        parts = jnp.concatenate([hi, mid, lo, jnp.zeros((5, ROWS), F32)], axis=0)
        parts = jnp.concatenate([parts[:, :D], parts[:, D:]], axis=0).astype(BF16)
        rows = tan_ref[pl.ds(pl.multiple_of(q_ref[0] * SUB, SUB), SUB), :]
        block = jnp.concatenate([rows, parts], axis=0)
        for i in range(DP):
            blk_ref[i] = block


def mass_pass(q, codes, tan):
    return pl.pallas_call(
        mass_kernel,
        grid=(LOCAL // WIDE,),
        in_specs=[
            SMEM,
            pl.BlockSpec((ROWS, WIDE), lambda c: (0, c)),
            pl.BlockSpec((ROWS, D), lambda c: (0, 0)),
        ],
        out_specs=pl.BlockSpec((DP, SUB + 16, D), lambda c: (0, 0, 0)),
        out_shape=jax.ShapeDtypeStruct((DP, SUB + 16, D), BF16),
        scratch_shapes=[pltpu.VMEM((ROWS, D), F32)],
        cost_estimate=pl.CostEstimate(flops=ROWS * LOCAL, bytes_accessed=5 << 20, transcendentals=0),
        compiler_params=pltpu.CompilerParams(vmem_limit_bytes=56 * MB),
        name="mass_pass",
    )(q, codes, tan)


def score_kernel(f_ref, tan_ref, a_ref, p_ref, codes_ref, e_ref, u_ref, cst_ref, st_ref, s_sc, t_sc, run, acc):
    step = pl.program_id(0)
    f = f_ref[...]
    s_sc[...] = lax.dot_general(f, a_ref[...], NT, preferred_element_type=F32)
    left = jnp.concatenate([tan_ref[...], f], axis=1)
    right = jnp.concatenate([a_ref[...], p_ref[...]], axis=1)
    t_sc[...] = lax.dot_general(left, right, NT, preferred_element_type=F32)

    @pl.when(step == 0)
    def _():
        run[0] = jnp.full((ROWS, D), -jnp.inf, F32)
        run[1] = jnp.zeros((ROWS, D), F32)
        run[2] = jnp.zeros((ROWS, D), F32)
        acc[...] = jnp.zeros_like(acc)

    acc[...] += jnp.dot(codes_ref[...], p_ref[...], preferred_element_type=F32)
    st_ref[:, D:] = acc[...]
    lane = lax.broadcasted_iota(jnp.int32, (RG, D), 1)
    for g in range(ROWS // RG):
        rows = slice(g * RG, (g + 1) * RG)
        s = s_sc[rows, :]
        t = t_sc[rows, :]
        top = jnp.max(s, axis=1, keepdims=True)
        e = jnp.exp2((s - top) * (INV * LOG2E))
        z = jnp.sum(e, axis=1, keepdims=True)
        et = jnp.sum(e * t, axis=1, keepdims=True)
        mean = et / z
        e_ref[rows, :] = e.astype(BF16)
        u_ref[rows, :] = (e * (t - mean)).astype(BF16)
        top = top * INV
        cst_ref[0, rows, :] = jnp.where(lane == 0, top, mean * INV)
        old = run[0, rows, :]
        new = jnp.maximum(old, top)
        alpha = jnp.exp(old - new)
        beta = jnp.exp(top - new)
        z_run = run[1, rows, :] * alpha + beta * z
        et_run = run[2, rows, :] * alpha + beta * (et * INV)
        run[0, rows, :] = new
        run[1, rows, :] = z_run
        run[2, rows, :] = et_run
        st_ref[rows, :D] = jnp.where(lane == 0, new, jnp.where(lane == 1, z_run, et_run))


def score_pass(f, tan, a, p, codes):
    return pl.pallas_call(
        score_kernel,
        grid=(NCH,),
        in_specs=[
            pl.BlockSpec((ROWS, D), lambda c: (0, 0)),
            pl.BlockSpec((ROWS, D), lambda c: (0, 0)),
            pl.BlockSpec((CN, D), lambda c: (c, 0)),
            pl.BlockSpec((CN, D), lambda c: (c, 0)),
            pl.BlockSpec((ROWS, CN), lambda c: (0, c)),
        ],
        out_specs=[
            pl.BlockSpec((ROWS, CN), lambda c: (0, c)),
            pl.BlockSpec((ROWS, CN), lambda c: (0, c)),
            pl.BlockSpec((1, ROWS, D), lambda c: (c, 0, 0)),
            pl.BlockSpec((ROWS, 2 * D), lambda c: (0, 0)),
        ],
        out_shape=[
            jax.ShapeDtypeStruct((ROWS, LOCAL), BF16),
            jax.ShapeDtypeStruct((ROWS, LOCAL), BF16),
            jax.ShapeDtypeStruct((NCH, ROWS, D), F32),
            jax.ShapeDtypeStruct((ROWS, 2 * D), F32),
        ],
        scratch_shapes=[
            pltpu.VMEM((ROWS, CN), F32),
            pltpu.VMEM((ROWS, CN), F32),
            pltpu.VMEM((3, ROWS, D), F32),
            pltpu.VMEM((ROWS, D), F32),
        ],
        cost_estimate=pl.CostEstimate(flops=10 * ROWS * LOCAL * D * 2, bytes_accessed=12 << 20, transcendentals=ROWS * LOCAL),
        compiler_params=pltpu.CompilerParams(vmem_limit_bytes=56 * MB),
        name="score_pass",
    )(f, tan, a, p, codes)


def embed_kernel(e_ref, u_ref, a_ref, p_ref, cst_ref, st_ref, x_ref, w_ref):
    @pl.when(pl.program_id(0) == 0)
    def _():
        x_ref[...] = jnp.zeros_like(x_ref)
        w_ref[...] = jnp.zeros_like(w_ref)

    e = e_ref[...]
    both = jnp.dot(e, jnp.concatenate([a_ref[...], p_ref[...]], axis=1), preferred_element_type=F32)
    ua = jnp.dot(u_ref[...], a_ref[...], preferred_element_type=F32)
    ea = both[:, :D]
    beta = jnp.exp(cst_ref[0, :, 0:1] - st_ref[:, 0:1])
    mean = cst_ref[0, :, 1:2]
    x_ref[...] += beta * (INV * ua + both[:, D:] + mean * ea)
    w_ref[...] += beta * ea


def embed_pass(e, u, a, p, cst, st):
    return pl.pallas_call(
        embed_kernel,
        grid=(NCH,),
        in_specs=[
            pl.BlockSpec((ROWS, CN), lambda c: (0, c)),
            pl.BlockSpec((ROWS, CN), lambda c: (0, c)),
            pl.BlockSpec((CN, D), lambda c: (c, 0)),
            pl.BlockSpec((CN, D), lambda c: (c, 0)),
            pl.BlockSpec((1, ROWS, D), lambda c: (c, 0, 0)),
            pl.BlockSpec((ROWS, D), lambda c: (0, 0)),
        ],
        out_specs=[
            pl.BlockSpec((ROWS, D), lambda c: (0, 0)),
            pl.BlockSpec((ROWS, D), lambda c: (0, 0)),
        ],
        out_shape=[jax.ShapeDtypeStruct((ROWS, D), F32)] * 2,
        cost_estimate=pl.CostEstimate(flops=6 * ROWS * LOCAL * D * 2, bytes_accessed=12 << 20, transcendentals=0),
        compiler_params=pltpu.CompilerParams(vmem_limit_bytes=56 * MB),
        name="embed_pass",
    )(e, u, a, p, cst, st)


STAT = 16
PAY = ROWS + 2 * STAT + SUB


def pick_kernel(q_ref, tab_ref, part_ref, st_ref, pay_ref):
    q = q_ref[0]
    partner = part_ref[...]
    group = partner // ROWS
    row = partner % ROWS
    mine = (row // SUB) == q
    column = jnp.where(mine, group * SUB + row % SUB, -1)
    hot = (lax.broadcasted_iota(jnp.int32, (ROWS, DP * SUB), 1) == column).astype(F32).astype(BF16)
    table = tab_ref[:, :SUB, :].reshape(DP * SUB, D)
    rows = jnp.dot(hot, table, preferred_element_type=F32).astype(BF16)

    hot_group = (lax.broadcasted_iota(jnp.int32, (ROWS, DP), 1) == group).astype(F32).astype(BF16)
    mass_rows = tab_ref[:, SUB:, :].astype(F32)
    mass = jnp.zeros((ROWS, ROWS), F32)
    for k in (2, 1, 0):
        piece = jnp.concatenate([mass_rows[:, k, :], mass_rows[:, 8 + k, :]], axis=1).astype(BF16)
        mass = mass + jnp.dot(hot_group, piece, preferred_element_type=F32)
    here = lax.broadcasted_iota(jnp.int32, (ROWS, ROWS), 1) == row
    mass = jnp.sum(jnp.where(here, mass, 0.0), axis=1, keepdims=True)

    lane = lax.broadcasted_iota(jnp.int32, (ROWS, D), 1)
    stats = jnp.where(lane == 3, mass, st_ref[:, :D])
    flat = jnp.transpose(stats)[:4, :]
    hi, mid, lo = split3(flat)
    flat = jnp.concatenate([hi, mid, lo, jnp.zeros((STAT - 12, ROWS), F32)], axis=0)
    flat = jnp.concatenate([flat[:, :D], flat[:, D:]], axis=0).astype(BF16)
    payload = jnp.concatenate([rows, flat], axis=0)
    for i in range(PR):
        pay_ref[i, : ROWS + 2 * STAT, :] = payload
        pay_ref[i, ROWS + 2 * STAT :, :] = st_ref[i * SUB : (i + 1) * SUB, D:].astype(BF16)


def pick(q, tab, partner, st):
    return pl.pallas_call(
        pick_kernel,
        in_specs=[SMEM, VMEM, VMEM, VMEM],
        out_specs=VMEM,
        out_shape=jax.ShapeDtypeStruct((PR, PAY, D), BF16),
        compiler_params=pltpu.CompilerParams(vmem_limit_bytes=10 * MB),
        name="pick",
    )(q, tab, partner, st)


def stats_kernel(rec_ref, f_ref, tan_ref, cst_ref, f12_ref, gst_ref, h_ref):
    total = jnp.zeros((ROWS, D), F32)
    h = jnp.zeros((SUB, D), F32)
    flats = []
    for i in range(PR):
        total = total + rec_ref[i, :ROWS, :].astype(F32)
        flat = rec_ref[i, ROWS : ROWS + 2 * STAT, :].astype(F32)
        flat = jnp.concatenate([flat[:STAT], flat[STAT:]], axis=1)
        flats.append((flat[0:4] + flat[4:8]) + flat[8:12])
        h = h + rec_ref[i, ROWS + 2 * STAT :, :].astype(F32)
    f12_ref[2 * NCH] = (total * SCALE).astype(BF16)
    h_ref[...] = h.astype(BF16)
    top = flats[0][0:1]
    for i in range(1, PR):
        top = jnp.maximum(top, flats[i][0:1])
    z = jnp.zeros((1, ROWS), F32)
    et = jnp.zeros((1, ROWS), F32)
    mass = jnp.zeros((1, ROWS), F32)
    for i in range(PR):
        shift = jnp.exp(flats[i][0:1] - top)
        z = z + shift * flats[i][1:2]
        et = et + shift * flats[i][2:3]
        mass = mass + flats[i][3:4]
    rows = jnp.concatenate([top, et / z, SCALE * mass / z, jnp.zeros((D - 3, ROWS), F32)], axis=0)
    cols = jnp.transpose(rows)
    gst_ref[...] = cols
    top = cols[:, 0:1]
    mean = cols[:, 1:2]
    weight = cols[:, 2:3]
    f = f_ref[...].astype(F32)
    tan = tan_ref[...].astype(F32)
    for c in range(NCH):
        scale = weight * jnp.exp(cst_ref[c, :, 0:1] - top)
        f12_ref[2 * c] = (INV * scale * f).astype(BF16)
        f12_ref[2 * c + 1] = (scale * ((cst_ref[c, :, 1:2] - mean) * f + tan)).astype(BF16)


def stats_pass(rec, f, tan, cst):
    return pl.pallas_call(
        stats_kernel,
        in_specs=[VMEM] * 4,
        out_specs=[VMEM] * 3,
        out_shape=[
            jax.ShapeDtypeStruct((2 * NCH + 1, ROWS, D), BF16),
            jax.ShapeDtypeStruct((ROWS, D), F32),
            jax.ShapeDtypeStruct((SUB, D), BF16),
        ],
        compiler_params=pltpu.CompilerParams(vmem_limit_bytes=10 * MB),
        name="stats_pass",
    )(rec, f, tan, cst)


def proto_kernel(s_ref, f12_ref, swt_ref, u_ref, e_ref, codes_ref, mine_ref, send_ref):
    res = lax.dot_general(u_ref[...], f12_ref[0], TN, preferred_element_type=F32)
    res = res + lax.dot_general(e_ref[...], f12_ref[1], TN, preferred_element_type=F32)
    res = res - lax.dot_general(codes_ref[...], swt_ref[0], TN, preferred_element_type=F32)
    first = s_ref[0] == 0
    for b in range(CN // (2 * ROWS)):
        even = res[2 * b * ROWS : (2 * b + 1) * ROWS]
        odd = res[(2 * b + 1) * ROWS : (2 * b + 2) * ROWS]
        mine_ref[b] = jnp.where(first, even, odd)
        send_ref[b] = jnp.where(first, odd, even).astype(BF16)


def proto_pass(scalars, f12, u, e, codes):
    nb = CN // (2 * ROWS)
    steps = NCH // 2
    wide = pl.BlockSpec((ROWS, CN), lambda c, s: (0, s[1] * steps + c))
    return pl.pallas_call(
        proto_kernel,
        grid_spec=pltpu.PrefetchScalarGridSpec(
            num_scalar_prefetch=1,
            grid=(steps,),
            in_specs=[
                pl.BlockSpec((2, ROWS, D), lambda c, s: (s[1] * steps + c, 0, 0)),
                pl.BlockSpec((1, ROWS, D), lambda c, s: (2 * NCH, 0, 0)),
                wide,
                wide,
                wide,
            ],
            out_specs=[
                pl.BlockSpec((nb, ROWS, D), lambda c, s: (c, 0, 0)),
                pl.BlockSpec((nb, ROWS, D), lambda c, s: (c, 0, 0)),
            ],
        ),
        out_shape=[
            jax.ShapeDtypeStruct((8, ROWS, D), F32),
            jax.ShapeDtypeStruct((8, ROWS, D), BF16),
        ],
        cost_estimate=pl.CostEstimate(flops=3 * ROWS * LOCAL * D * 2, bytes_accessed=9 << 20, transcendentals=0),
        compiler_params=pltpu.CompilerParams(vmem_limit_bytes=56 * MB),
        name="proto_pass",
    )(scalars, f12, f12, u, e, codes)


def final_kernel(pieces_ref, out_ref):
    total = pieces_ref[0].astype(F32)
    for i in range(1, 8):
        total = total + pieces_ref[i].astype(F32)
    total = total.astype(BF16)
    for i in range(8):
        out_ref[i] = total


def final_pass(pieces):
    return pl.pallas_call(
        final_kernel,
        in_specs=[VMEM],
        out_specs=VMEM,
        out_shape=jax.ShapeDtypeStruct((8, ROWS, D), BF16),
        compiler_params=pltpu.CompilerParams(vmem_limit_bytes=8 * MB),
        name="final_pass",
    )(pieces)


def row_kernel(s_ref, own_ref, other_ref, part_ref, x_ref, w_ref, st_ref, gst_ref, emb_ref):
    q = s_ref[0]
    partner = part_ref[...]
    away = (partner // ROWS) ^ s_ref[1]
    block = (away & 1) + 2 * ((away >> 3) & 1) + 4 * ((away >> 2) & 1) + 8 * ((away >> 1) & 1) + 16 * ((away >> 4) & 1)
    row = partner % ROWS
    column = jnp.where((row // SUB) == q, block * SUB + row % SUB, -1)
    hot = (lax.broadcasted_iota(jnp.int32, (ROWS, DP * SUB), 1) == column).astype(F32).astype(BF16)
    table = jnp.concatenate([own_ref[...], other_ref[...]], axis=0)
    h = jnp.dot(hot, table, preferred_element_type=F32)
    scale = gst_ref[:, 2:3] * jnp.exp(st_ref[:, 0:1] - gst_ref[:, 0:1])
    emb_ref[...] = scale * (x_ref[...] - gst_ref[:, 1:2] * w_ref[...]) - SCALE * h


def row_pass(scalars, own, other, partner, x, w, st, gst):
    return pl.pallas_call(
        row_kernel,
        in_specs=[SMEM] + [VMEM] * 7,
        out_specs=VMEM,
        out_shape=jax.ShapeDtypeStruct((ROWS, D), F32),
        compiler_params=pltpu.CompilerParams(vmem_limit_bytes=8 * MB),
        name="row_pass",
    )(scalars, own, other, partner, x, w, st, gst)


def place_kernel(pieces, s_ref, *refs):
    out_ref, sems = refs[-2], refs[-1]
    copies = []
    for ref, (far, other, first) in zip(refs, pieces):
        for i in range(0, ref.shape[0], 2):
            copies.append(pltpu.make_async_copy(
                ref.at[i : i + 2],
                out_ref.at[s_ref[0] ^ far, first + i : first + i + 2, s_ref[1] ^ other],
                sems.at[len(copies)],
            ))
    for copy in copies:
        copy.start()
    for copy in copies:
        copy.wait()


def place(scalars, pieces, blocks, whole):
    rest = () if whole is None else (whole,)
    count = sum(block.shape[0] // 2 for block in blocks)
    return pl.pallas_call(
        functools.partial(place_kernel, pieces),
        in_specs=[SMEM] + [VMEM] * len(blocks) + [HBM] * len(rest),
        out_specs=HBM,
        out_shape=jax.ShapeDtypeStruct((2, 8, 2, ROWS, D), BF16),
        scratch_shapes=[pltpu.SemaphoreType.DMA((count,))],
        input_output_aliases={1 + len(blocks): 0} if rest else {},
        compiler_params=pltpu.CompilerParams(vmem_limit_bytes=4 * MB),
        name="place",
    )(scalars, *blocks, *rest)


CORE_PERM = [(i, i ^ 1) for i in range(DP)]
Y_PERM = [(i, i ^ 16) for i in range(DP)]
Z_GROUPS = [[y * 16 + z * 2 + c for z in range(8)] for y in range(2) for c in range(2)]


def exchange(x, axis, groups=None):
    return lax.all_to_all(x, axis, 0, 0, axis_index_groups=groups, tiled=True)


def doubled(x, bit):
    other = lax.ppermute(x, "dp", [(i, i ^ bit) for i in range(DP)])
    return lax.optimization_barrier(jnp.concatenate([x, other], axis=0))


def swap(x, bit):
    return lax.ppermute(x, "proto", [(i, i ^ bit) for i in range(PR)])


def inner(feature_matrix, tangent_embed, anchor_matrix, anchor_perturbation, codes, partner_lookup):
    dp = lax.axis_index("dp")
    q = lax.axis_index("proto")
    core = dp % 2
    y = dp // 16
    partner = partner_lookup.reshape(ROWS, 1)
    qs = q.reshape(1)

    block = mass_pass(qs, codes, tangent_embed)
    table = exchange(block, "dp")
    e, u, cst, st = score_pass(feature_matrix, tangent_embed, anchor_matrix, anchor_perturbation, codes)

    received = exchange(pick(qs, table, partner, st), "proto")
    x, w = embed_pass(e, u, anchor_matrix, anchor_perturbation, cst, st)
    received, x, w = lax.optimization_barrier((received, x, w))
    f12, gst, h_own = stats_pass(received, feature_matrix, tangent_embed, cst)

    table = doubled(h_own, 1)
    mine_far, send_far = proto_pass(jnp.stack([core, 1 - y]), f12, u, e, codes)
    table = doubled(table, 8)
    got_far = lax.ppermute(send_far, "dp", CORE_PERM)
    to_y = (mine_far + got_far.astype(F32)).astype(BF16)
    from_far = lax.ppermute(to_y, "dp", Y_PERM)
    f12, to_y = lax.optimization_barrier((f12, to_y))
    table = doubled(table, 4)
    mine_near, send_near = proto_pass(jnp.stack([core, y]), f12, u, e, codes)
    got_near = lax.ppermute(send_near, "dp", CORE_PERM)
    table = doubled(table, 2)
    near = lax.optimization_barrier(mine_near + got_near.astype(F32))
    quarter = (near + from_far.astype(F32)).astype(BF16)
    pieces = exchange(quarter, "dp", Z_GROUPS)
    other = lax.ppermute(table, "dp", Y_PERM)
    embed = row_pass(jnp.stack([q, dp]), table, other, partner, x, w, st, gst)
    final = final_pass(pieces)

    swapped = swap(embed, 1)
    along_z = exchange(final, "dp", Z_GROUPS)
    far_a = lax.ppermute(along_z[:4], "dp", Y_PERM)
    far_b = lax.ppermute(along_z[4:], "dp", Y_PERM)
    embed = embed + swapped
    swapped = swap(embed, 4)
    embed = embed + swapped
    swapped = swap(embed, 2)
    hvp_embed = (embed + swapped).astype(BF16)
    own_core = lax.ppermute(along_z, "dp", CORE_PERM)
    core_a = lax.ppermute(far_a, "dp", CORE_PERM)
    core_b = lax.ppermute(far_b, "dp", CORE_PERM)
    where = jnp.stack([y, core])
    whole = place(where, ((0, 0, 0), (0, 1, 0)), (along_z, own_core), None)
    whole = place(where, ((1, 0, 0), (1, 1, 0)), (far_a, core_a), whole)
    whole = place(where, ((1, 0, 4), (1, 1, 4)), (far_b, core_b), whole)
    return (hvp_embed, whole.reshape(LOCAL, D))


def solution(mesh):
    in_specs = (
        P("dp", None),
        P("dp", None),
        P("proto", None),
        P("proto", None),
        P("dp", "proto"),
        P("dp"),
    )
    out_specs = (P("dp", None), P("proto", None))
    return jax.shard_map(inner, mesh=mesh, in_specs=in_specs, out_specs=out_specs, check_vma=False)
```

```python
import functools

import jax
import jax.numpy as jnp
from jax import lax
from jax.experimental import pallas as pl
from jax.experimental.pallas import tpu as pltpu
from jax.sharding import PartitionSpec as P


F32 = jnp.float32
BF16 = jnp.bfloat16
NT = (((1,), (1,)), ((), ()))
TN = (((0,), (0,)), ((), ()))
D = 128
ROWS = 256
LOCAL = 8192
DP = 32
PR = 8
SUB = ROWS // PR
CN = 2048
NCH = LOCAL // CN
SCALE = 0.1
RG = 16
INV = 10.0
LOG2E = 1.4426950408889634
VMEM = pl.BlockSpec(memory_space=pltpu.VMEM)
SMEM = pl.BlockSpec(memory_space=pltpu.SMEM)
HBM = pl.BlockSpec(memory_space=pltpu.HBM)
MB = 1024 * 1024


def split3(x):
    hi = x.astype(BF16).astype(F32)
    mid = (x - hi).astype(BF16).astype(F32)
    lo = (x - hi - mid).astype(BF16).astype(F32)
    return hi, mid, lo


WIDE = 4096


def mass_kernel(q_ref, codes_ref, tan_ref, blk_ref, acc):
    step = pl.program_id(0)

    @pl.when(step == 0)
    def _():
        acc[...] = jnp.zeros_like(acc)

    for g in range(ROWS // RG):
        rows = slice(g * RG, (g + 1) * RG)
        x = codes_ref[rows, :].astype(F32)
        total = x[:, :D]
        for k in range(1, WIDE // D):
            total = total + x[:, k * D : (k + 1) * D]
        acc[rows, :] += total

    @pl.when(step == LOCAL // WIDE - 1)
    def _():
        mass = jnp.sum(jnp.transpose(acc[...]), axis=0, keepdims=True)
        hi, mid, lo = split3(mass)
        parts = jnp.concatenate([hi, mid, lo, jnp.zeros((5, ROWS), F32)], axis=0)
        parts = jnp.concatenate([parts[:, :D], parts[:, D:]], axis=0).astype(BF16)
        rows = tan_ref[pl.ds(pl.multiple_of(q_ref[0] * SUB, SUB), SUB), :]
        block = jnp.concatenate([rows, parts], axis=0)
        for i in range(DP):
            blk_ref[i] = block


def mass_pass(q, codes, tan):
    return pl.pallas_call(
        mass_kernel,
        grid=(LOCAL // WIDE,),
        in_specs=[
            SMEM,
            pl.BlockSpec((ROWS, WIDE), lambda c: (0, c)),
            pl.BlockSpec((ROWS, D), lambda c: (0, 0)),
        ],
        out_specs=pl.BlockSpec((DP, SUB + 16, D), lambda c: (0, 0, 0)),
        out_shape=jax.ShapeDtypeStruct((DP, SUB + 16, D), BF16),
        scratch_shapes=[pltpu.VMEM((ROWS, D), F32)],
        cost_estimate=pl.CostEstimate(flops=ROWS * LOCAL, bytes_accessed=5 << 20, transcendentals=0),
        compiler_params=pltpu.CompilerParams(vmem_limit_bytes=56 * MB),
        name="mass_pass",
    )(q, codes, tan)


def score_kernel(f_ref, tan_ref, a_ref, p_ref, codes_ref, e_ref, u_ref, cst_ref, st_ref, s_sc, t_sc, run, acc):
    step = pl.program_id(0)
    f = f_ref[...]
    s_sc[...] = lax.dot_general(f, a_ref[...], NT, preferred_element_type=F32)
    left = jnp.concatenate([tan_ref[...], f], axis=1)
    right = jnp.concatenate([a_ref[...], p_ref[...]], axis=1)
    t_sc[...] = lax.dot_general(left, right, NT, preferred_element_type=F32)

    @pl.when(step == 0)
    def _():
        run[0] = jnp.full((ROWS, D), -jnp.inf, F32)
        run[1] = jnp.zeros((ROWS, D), F32)
        run[2] = jnp.zeros((ROWS, D), F32)
        acc[...] = jnp.zeros_like(acc)

    acc[...] += jnp.dot(codes_ref[...], p_ref[...], preferred_element_type=F32)
    st_ref[:, D:] = acc[...]
    lane = lax.broadcasted_iota(jnp.int32, (RG, D), 1)
    for g in range(ROWS // RG):
        rows = slice(g * RG, (g + 1) * RG)
        s = s_sc[rows, :]
        t = t_sc[rows, :]
        top = jnp.max(s, axis=1, keepdims=True)
        e = jnp.exp2((s - top) * (INV * LOG2E))
        z = jnp.sum(e, axis=1, keepdims=True)
        et = jnp.sum(e * t, axis=1, keepdims=True)
        mean = et / z
        e_ref[rows, :] = e.astype(BF16)
        u_ref[rows, :] = (e * (t - mean)).astype(BF16)
        top = top * INV
        cst_ref[0, rows, :] = jnp.where(lane == 0, top, mean * INV)
        old = run[0, rows, :]
        new = jnp.maximum(old, top)
        alpha = jnp.exp(old - new)
        beta = jnp.exp(top - new)
        z_run = run[1, rows, :] * alpha + beta * z
        et_run = run[2, rows, :] * alpha + beta * (et * INV)
        run[0, rows, :] = new
        run[1, rows, :] = z_run
        run[2, rows, :] = et_run
        st_ref[rows, :D] = jnp.where(lane == 0, new, jnp.where(lane == 1, z_run, et_run))


def score_pass(f, tan, a, p, codes):
    return pl.pallas_call(
        score_kernel,
        grid=(NCH,),
        in_specs=[
            pl.BlockSpec((ROWS, D), lambda c: (0, 0)),
            pl.BlockSpec((ROWS, D), lambda c: (0, 0)),
            pl.BlockSpec((CN, D), lambda c: (c, 0)),
            pl.BlockSpec((CN, D), lambda c: (c, 0)),
            pl.BlockSpec((ROWS, CN), lambda c: (0, c)),
        ],
        out_specs=[
            pl.BlockSpec((ROWS, CN), lambda c: (0, c)),
            pl.BlockSpec((ROWS, CN), lambda c: (0, c)),
            pl.BlockSpec((1, ROWS, D), lambda c: (c, 0, 0)),
            pl.BlockSpec((ROWS, 2 * D), lambda c: (0, 0)),
        ],
        out_shape=[
            jax.ShapeDtypeStruct((ROWS, LOCAL), BF16),
            jax.ShapeDtypeStruct((ROWS, LOCAL), BF16),
            jax.ShapeDtypeStruct((NCH, ROWS, D), F32),
            jax.ShapeDtypeStruct((ROWS, 2 * D), F32),
        ],
        scratch_shapes=[
            pltpu.VMEM((ROWS, CN), F32),
            pltpu.VMEM((ROWS, CN), F32),
            pltpu.VMEM((3, ROWS, D), F32),
            pltpu.VMEM((ROWS, D), F32),
        ],
        cost_estimate=pl.CostEstimate(flops=10 * ROWS * LOCAL * D * 2, bytes_accessed=12 << 20, transcendentals=ROWS * LOCAL),
        compiler_params=pltpu.CompilerParams(vmem_limit_bytes=51 * MB),
        name="score_pass",
    )(f, tan, a, p, codes)


def embed_kernel(e_ref, u_ref, a_ref, p_ref, cst_ref, st_ref, x_ref, w_ref):
    @pl.when(pl.program_id(0) == 0)
    def _():
        x_ref[...] = jnp.zeros_like(x_ref)
        w_ref[...] = jnp.zeros_like(w_ref)

    e = e_ref[...]
    both = jnp.dot(e, jnp.concatenate([a_ref[...], p_ref[...]], axis=1), preferred_element_type=F32)
    ua = jnp.dot(u_ref[...], a_ref[...], preferred_element_type=F32)
    ea = both[:, :D]
    beta = jnp.exp(cst_ref[0, :, 0:1] - st_ref[:, 0:1])
    mean = cst_ref[0, :, 1:2]
    x_ref[...] += beta * (INV * ua + both[:, D:] + mean * ea)
    w_ref[...] += beta * ea


def embed_pass(e, u, a, p, cst, st):
    return pl.pallas_call(
        embed_kernel,
        grid=(NCH,),
        in_specs=[
            pl.BlockSpec((ROWS, CN), lambda c: (0, c)),
            pl.BlockSpec((ROWS, CN), lambda c: (0, c)),
            pl.BlockSpec((CN, D), lambda c: (c, 0)),
            pl.BlockSpec((CN, D), lambda c: (c, 0)),
            pl.BlockSpec((1, ROWS, D), lambda c: (c, 0, 0)),
            pl.BlockSpec((ROWS, D), lambda c: (0, 0)),
        ],
        out_specs=[
            pl.BlockSpec((ROWS, D), lambda c: (0, 0)),
            pl.BlockSpec((ROWS, D), lambda c: (0, 0)),
        ],
        out_shape=[jax.ShapeDtypeStruct((ROWS, D), F32)] * 2,
        cost_estimate=pl.CostEstimate(flops=6 * ROWS * LOCAL * D * 2, bytes_accessed=12 << 20, transcendentals=0),
        compiler_params=pltpu.CompilerParams(vmem_limit_bytes=51 * MB),
        name="embed_pass",
    )(e, u, a, p, cst, st)


STAT = 16
PAY = ROWS + 2 * STAT + SUB


def pick_kernel(q_ref, tab_ref, part_ref, st_ref, pay_ref):
    q = q_ref[0]
    partner = part_ref[...]
    group = partner // ROWS
    row = partner % ROWS
    mine = (row // SUB) == q
    column = jnp.where(mine, group * SUB + row % SUB, -1)
    hot = (lax.broadcasted_iota(jnp.int32, (ROWS, DP * SUB), 1) == column).astype(F32).astype(BF16)
    table = tab_ref[:, :SUB, :].reshape(DP * SUB, D)
    rows = jnp.dot(hot, table, preferred_element_type=F32).astype(BF16)

    hot_group = (lax.broadcasted_iota(jnp.int32, (ROWS, DP), 1) == group).astype(F32).astype(BF16)
    mass_rows = tab_ref[:, SUB:, :].astype(F32)
    mass = jnp.zeros((ROWS, ROWS), F32)
    for k in (2, 1, 0):
        piece = jnp.concatenate([mass_rows[:, k, :], mass_rows[:, 8 + k, :]], axis=1).astype(BF16)
        mass = mass + jnp.dot(hot_group, piece, preferred_element_type=F32)
    here = lax.broadcasted_iota(jnp.int32, (ROWS, ROWS), 1) == row
    mass = jnp.sum(jnp.where(here, mass, 0.0), axis=1, keepdims=True)

    lane = lax.broadcasted_iota(jnp.int32, (ROWS, D), 1)
    stats = jnp.where(lane == 3, mass, st_ref[:, :D])
    flat = jnp.transpose(stats)[:4, :]
    hi, mid, lo = split3(flat)
    flat = jnp.concatenate([hi, mid, lo, jnp.zeros((STAT - 12, ROWS), F32)], axis=0)
    flat = jnp.concatenate([flat[:, :D], flat[:, D:]], axis=0).astype(BF16)
    payload = jnp.concatenate([rows, flat], axis=0)
    for i in range(PR):
        pay_ref[i, : ROWS + 2 * STAT, :] = payload
        pay_ref[i, ROWS + 2 * STAT :, :] = st_ref[i * SUB : (i + 1) * SUB, D:].astype(BF16)


def pick(q, tab, partner, st):
    return pl.pallas_call(
        pick_kernel,
        in_specs=[SMEM, VMEM, VMEM, VMEM],
        out_specs=VMEM,
        out_shape=jax.ShapeDtypeStruct((PR, PAY, D), BF16),
        compiler_params=pltpu.CompilerParams(vmem_limit_bytes=10 * MB),
        name="pick",
    )(q, tab, partner, st)


def stats_kernel(rec_ref, f_ref, tan_ref, cst_ref, f12_ref, gst_ref, h_ref):
    total = jnp.zeros((ROWS, D), F32)
    h = jnp.zeros((SUB, D), F32)
    flats = []
    for i in range(PR):
        total = total + rec_ref[i, :ROWS, :].astype(F32)
        flat = rec_ref[i, ROWS : ROWS + 2 * STAT, :].astype(F32)
        flat = jnp.concatenate([flat[:STAT], flat[STAT:]], axis=1)
        flats.append((flat[0:4] + flat[4:8]) + flat[8:12])
        h = h + rec_ref[i, ROWS + 2 * STAT :, :].astype(F32)
    f12_ref[2 * NCH] = (total * SCALE).astype(BF16)
    h_ref[...] = h.astype(BF16)
    top = flats[0][0:1]
    for i in range(1, PR):
        top = jnp.maximum(top, flats[i][0:1])
    z = jnp.zeros((1, ROWS), F32)
    et = jnp.zeros((1, ROWS), F32)
    mass = jnp.zeros((1, ROWS), F32)
    for i in range(PR):
        shift = jnp.exp(flats[i][0:1] - top)
        z = z + shift * flats[i][1:2]
        et = et + shift * flats[i][2:3]
        mass = mass + flats[i][3:4]
    rows = jnp.concatenate([top, et / z, SCALE * mass / z, jnp.zeros((D - 3, ROWS), F32)], axis=0)
    cols = jnp.transpose(rows)
    gst_ref[...] = cols
    top = cols[:, 0:1]
    mean = cols[:, 1:2]
    weight = cols[:, 2:3]
    f = f_ref[...].astype(F32)
    tan = tan_ref[...].astype(F32)
    for c in range(NCH):
        scale = weight * jnp.exp(cst_ref[c, :, 0:1] - top)
        f12_ref[2 * c] = (INV * scale * f).astype(BF16)
        f12_ref[2 * c + 1] = (scale * ((cst_ref[c, :, 1:2] - mean) * f + tan)).astype(BF16)


def stats_pass(rec, f, tan, cst):
    return pl.pallas_call(
        stats_kernel,
        in_specs=[VMEM] * 4,
        out_specs=[VMEM] * 3,
        out_shape=[
            jax.ShapeDtypeStruct((2 * NCH + 1, ROWS, D), BF16),
            jax.ShapeDtypeStruct((ROWS, D), F32),
            jax.ShapeDtypeStruct((SUB, D), BF16),
        ],
        compiler_params=pltpu.CompilerParams(vmem_limit_bytes=10 * MB),
        name="stats_pass",
    )(rec, f, tan, cst)


def proto_kernel(s_ref, f12_ref, swt_ref, u_ref, e_ref, codes_ref, mine_ref, send_ref):
    res = lax.dot_general(u_ref[...], f12_ref[0], TN, preferred_element_type=F32)
    res = res + lax.dot_general(e_ref[...], f12_ref[1], TN, preferred_element_type=F32)
    res = res - lax.dot_general(codes_ref[...], swt_ref[0], TN, preferred_element_type=F32)
    first = s_ref[0] == 0
    for b in range(CN // (2 * ROWS)):
        even = res[2 * b * ROWS : (2 * b + 1) * ROWS]
        odd = res[(2 * b + 1) * ROWS : (2 * b + 2) * ROWS]
        mine_ref[b] = jnp.where(first, even, odd)
        send_ref[b] = jnp.where(first, odd, even).astype(BF16)


def proto_pass(scalars, f12, u, e, codes):
    nb = CN // (2 * ROWS)
    steps = NCH // 2
    wide = pl.BlockSpec((ROWS, CN), lambda c, s: (0, s[1] * steps + c))
    return pl.pallas_call(
        proto_kernel,
        grid_spec=pltpu.PrefetchScalarGridSpec(
            num_scalar_prefetch=1,
            grid=(steps,),
            in_specs=[
                pl.BlockSpec((2, ROWS, D), lambda c, s: (s[1] * steps + c, 0, 0)),
                pl.BlockSpec((1, ROWS, D), lambda c, s: (2 * NCH, 0, 0)),
                wide,
                wide,
                wide,
            ],
            out_specs=[
                pl.BlockSpec((nb, ROWS, D), lambda c, s: (c, 0, 0)),
                pl.BlockSpec((nb, ROWS, D), lambda c, s: (c, 0, 0)),
            ],
        ),
        out_shape=[
            jax.ShapeDtypeStruct((8, ROWS, D), F32),
            jax.ShapeDtypeStruct((8, ROWS, D), BF16),
        ],
        cost_estimate=pl.CostEstimate(flops=3 * ROWS * LOCAL * D * 2, bytes_accessed=9 << 20, transcendentals=0),
        compiler_params=pltpu.CompilerParams(vmem_limit_bytes=51 * MB),
        name="proto_pass",
    )(scalars, f12, f12, u, e, codes)


def final_kernel(pieces_ref, out_ref):
    total = pieces_ref[0].astype(F32)
    for i in range(1, 8):
        total = total + pieces_ref[i].astype(F32)
    total = total.astype(BF16)
    for i in range(8):
        out_ref[i] = total


def final_pass(pieces):
    return pl.pallas_call(
        final_kernel,
        in_specs=[VMEM],
        out_specs=VMEM,
        out_shape=jax.ShapeDtypeStruct((8, ROWS, D), BF16),
        compiler_params=pltpu.CompilerParams(vmem_limit_bytes=8 * MB),
        name="final_pass",
    )(pieces)


def row_kernel(s_ref, own_ref, other_ref, part_ref, x_ref, w_ref, st_ref, gst_ref, emb_ref):
    q = s_ref[0]
    partner = part_ref[...]
    away = (partner // ROWS) ^ s_ref[1]
    block = (away & 1) + 2 * ((away >> 3) & 1) + 4 * ((away >> 2) & 1) + 8 * ((away >> 1) & 1) + 16 * ((away >> 4) & 1)
    row = partner % ROWS
    column = jnp.where((row // SUB) == q, block * SUB + row % SUB, -1)
    hot = (lax.broadcasted_iota(jnp.int32, (ROWS, DP * SUB), 1) == column).astype(F32).astype(BF16)
    table = jnp.concatenate([own_ref[...], other_ref[...]], axis=0)
    h = jnp.dot(hot, table, preferred_element_type=F32)
    scale = gst_ref[:, 2:3] * jnp.exp(st_ref[:, 0:1] - gst_ref[:, 0:1])
    emb_ref[...] = scale * (x_ref[...] - gst_ref[:, 1:2] * w_ref[...]) - SCALE * h


def row_pass(scalars, own, other, partner, x, w, st, gst):
    return pl.pallas_call(
        row_kernel,
        in_specs=[SMEM] + [VMEM] * 7,
        out_specs=VMEM,
        out_shape=jax.ShapeDtypeStruct((ROWS, D), F32),
        compiler_params=pltpu.CompilerParams(vmem_limit_bytes=8 * MB),
        name="row_pass",
    )(scalars, own, other, partner, x, w, st, gst)


def place_kernel(pieces, s_ref, *refs):
    out_ref, sems = refs[-2], refs[-1]
    copies = []
    for ref, (far, other, first) in zip(refs, pieces):
        for i in range(0, ref.shape[0], 2):
            copies.append(pltpu.make_async_copy(
                ref.at[i : i + 2],
                out_ref.at[s_ref[0] ^ far, first + i : first + i + 2, s_ref[1] ^ other],
                sems.at[len(copies)],
            ))
    for copy in copies:
        copy.start()
    for copy in copies:
        copy.wait()


def place(scalars, pieces, blocks, whole):
    rest = () if whole is None else (whole,)
    count = sum(block.shape[0] // 2 for block in blocks)
    return pl.pallas_call(
        functools.partial(place_kernel, pieces),
        in_specs=[SMEM] + [VMEM] * len(blocks) + [HBM] * len(rest),
        out_specs=HBM,
        out_shape=jax.ShapeDtypeStruct((2, 8, 2, ROWS, D), BF16),
        scratch_shapes=[pltpu.SemaphoreType.DMA((count,))],
        input_output_aliases={1 + len(blocks): 0} if rest else {},
        compiler_params=pltpu.CompilerParams(vmem_limit_bytes=4 * MB),
        name="place",
    )(scalars, *blocks, *rest)


CORE_PERM = [(i, i ^ 1) for i in range(DP)]
Y_PERM = [(i, i ^ 16) for i in range(DP)]
Z_GROUPS = [[y * 16 + z * 2 + c for z in range(8)] for y in range(2) for c in range(2)]


def exchange(x, axis, groups=None):
    return lax.all_to_all(x, axis, 0, 0, axis_index_groups=groups, tiled=True)


def doubled(x, bit):
    other = lax.ppermute(x, "dp", [(i, i ^ bit) for i in range(DP)])
    return lax.optimization_barrier(jnp.concatenate([x, other], axis=0))


def swap(x, bit):
    return lax.ppermute(x, "proto", [(i, i ^ bit) for i in range(PR)])


def inner(feature_matrix, tangent_embed, anchor_matrix, anchor_perturbation, codes, partner_lookup):
    dp = lax.axis_index("dp")
    q = lax.axis_index("proto")
    core = dp % 2
    y = dp // 16
    partner = partner_lookup.reshape(ROWS, 1)
    qs = q.reshape(1)

    block = mass_pass(qs, codes, tangent_embed)
    table = exchange(block, "dp")
    e, u, cst, st = score_pass(feature_matrix, tangent_embed, anchor_matrix, anchor_perturbation, codes)

    received = exchange(pick(qs, table, partner, st), "proto")
    x, w = embed_pass(e, u, anchor_matrix, anchor_perturbation, cst, st)
    received, x, w = lax.optimization_barrier((received, x, w))
    f12, gst, h_own = stats_pass(received, feature_matrix, tangent_embed, cst)

    table = doubled(h_own, 1)
    mine_far, send_far = proto_pass(jnp.stack([core, 1 - y]), f12, u, e, codes)
    table = doubled(table, 8)
    got_far = lax.ppermute(send_far, "dp", CORE_PERM)
    to_y = (mine_far + got_far.astype(F32)).astype(BF16)
    from_far = lax.ppermute(to_y, "dp", Y_PERM)
    f12, to_y = lax.optimization_barrier((f12, to_y))
    table = doubled(table, 4)
    mine_near, send_near = proto_pass(jnp.stack([core, y]), f12, u, e, codes)
    got_near = lax.ppermute(send_near, "dp", CORE_PERM)
    table = doubled(table, 2)
    near = lax.optimization_barrier(mine_near + got_near.astype(F32))
    quarter = (near + from_far.astype(F32)).astype(BF16)
    pieces = exchange(quarter, "dp", Z_GROUPS)
    other = lax.ppermute(table, "dp", Y_PERM)
    embed = row_pass(jnp.stack([q, dp]), table, other, partner, x, w, st, gst)
    final = final_pass(pieces)

    swapped = swap(embed, 1)
    along_z = exchange(final, "dp", Z_GROUPS)
    far_a = lax.ppermute(along_z[:4], "dp", Y_PERM)
    far_b = lax.ppermute(along_z[4:], "dp", Y_PERM)
    embed = embed + swapped
    swapped = swap(embed, 4)
    embed = embed + swapped
    swapped = swap(embed, 2)
    hvp_embed = (embed + swapped).astype(BF16)
    own_core = lax.ppermute(along_z, "dp", CORE_PERM)
    core_a = lax.ppermute(far_a, "dp", CORE_PERM)
    core_b = lax.ppermute(far_b, "dp", CORE_PERM)
    where = jnp.stack([y, core])
    whole = place(where, ((0, 0, 0), (0, 1, 0)), (along_z, own_core), None)
    whole = place(where, ((1, 0, 0), (1, 1, 0)), (far_a, core_a), whole)
    whole = place(where, ((1, 0, 4), (1, 1, 4)), (far_b, core_b), whole)
    return (hvp_embed, whole.reshape(LOCAL, D))


def solution(mesh):
    in_specs = (
        P("dp", None),
        P("dp", None),
        P("proto", None),
        P("proto", None),
        P("dp", "proto"),
        P("dp"),
    )
    out_specs = (P("dp", None), P("proto", None))
    return jax.shard_map(inner, mesh=mesh, in_specs=in_specs, out_specs=out_specs, check_vma=False)
```
